32 devices in a mesh: seg: 4 (over z), mpo: 4 (over x, core), sec: 2 (over y).
Axes of the slice: x: 2, y: 2, z: 4, core: 2. Of those that a mesh axis runs over, the one named last changes fastest.
Arguments:
- state: bfloat16 [4, 1024, 1024], P('seg', 'sec'), may hold values from -6 to 6
- left_env: bfloat16 [4, 12, 1024, 1024], P('seg', 'mpo', 'sec'), may hold values from -0.1875 to 0.1875
- right_env: bfloat16 [4, 12, 1024, 1024], P('seg', 'mpo'), may hold values from -0.1875 to 0.1875
- inv_singular: float32 [4, 1024], P('seg'), may hold values from 0.5 to 2
- sketch_cols: bfloat16 [4, 2, 1024, 256], P('seg'), may hold values from -6 to 6
- kept_ranks: int32 [4], P('seg'), may hold values from 128 to 256, as said below
Outputs:
- final_state: bfloat16 [4, 1024, 1024], P('seg', 'sec')
The draws below stay inside these ranges and needn't reach their ends.
Inputs may be any that keep to these rules, and one draw needn't show every extreme that they name: `kept_ranks`: each segment keeps between 128 and 256 ranks; some segment keeps exactly 256.
All inputs are finite; a program needn't handle non-finite values.
Results may differ from the reference program's by a relative error of at most 0.025.
Values may be sent and summed in bfloat16 or wider, within the bound.
No kernel may reach another device: no remote copies, remote signals or barrier semaphores. Data moves between devices by JAX's collectives and lax.ppermute only.
A program may use at most 128 MiB of HBM per device.

```python
import math
import jax
import jax.numpy as jnp
from jax import lax

D = 1024
P_SIZE = 256
ITERS = 2
MPO_TERMS = 12
SEGS = 4


def draw_kept_ranks(key, part):
    first_key, second_key = jax.random.split(key)
    ranks = jax.random.randint(first_key, (SEGS,), P_SIZE // 2, P_SIZE + 1)
    where = jax.random.randint(second_key, (), 0, SEGS)
    return ranks.at[where].set(P_SIZE).astype(jnp.int32)


def block_scale(own_key, shape, pieces, low, largest):
    def one(axis_at, blocks):
        steps = jax.random.uniform(jax.random.fold_in(jax.random.fold_in(own_key, 6), axis_at), (blocks,), jnp.float32, low / len(pieces), largest / len(pieces))
        return jnp.repeat(jnp.exp(steps), shape[axis_at] // blocks).reshape((-1,) + (1,) * (len(shape) - axis_at - 1))

    factor_of = one(*pieces[0])
    for cut in pieces[1:]:
        factor_of = factor_of * one(*cut)
    return factor_of


def scatter_about(rng, extent, width, limit, pieces=(), kind=jnp.bfloat16):
    drawn = width * jax.random.normal(rng, extent, jnp.float32)
    if pieces:
        drawn = drawn * block_scale(rng, extent, pieces, -0.22, 0.18)
    return jnp.clip(drawn, -limit, limit).astype(kind)


def setup_inputs(seed: int = 0) -> dict:
    seeds = jax.random.split(jax.random.key(seed), 7)
    return {
        "state": scatter_about(seeds[0], (SEGS, D, D), 1.0, 6.0, ((0, 4), (1, 2))),
        "left_env": scatter_about(seeds[1], (SEGS, MPO_TERMS, D, D), D ** -0.5, 0.1875, ((0, 4), (1, 4), (2, 2))),
        "right_env": scatter_about(seeds[2], (SEGS, MPO_TERMS, D, D), D ** -0.5, 0.1875, ((0, 4), (1, 4))),
        "inv_singular": jnp.clip(jnp.exp(math.log(2.0) - 1.3862944 * jax.random.uniform(seeds[3], (SEGS, D), jnp.float32) ** block_scale(seeds[3], (SEGS, D), ((0, 4),), -0.2, 0.2)), 0.5, 2.0),
        "sketch_cols": scatter_about(seeds[4], (SEGS, 2, D, P_SIZE), 1.0, 6.0, ((0, 4),)),
        "kept_ranks": draw_kept_ranks(jax.random.fold_in(seeds[6], 71), 0),
    }


TAU = 0.3
MOMENTUM = 0.5
EPS = 1e-06

def gradient_step(y, previous, left, right):

    def add_term(total, pair):
        left_k, right_k = pair
        first = jnp.dot(left_k.astype(jnp.float32), y.astype(jnp.float32), preferred_element_type=jnp.float32).astype(jnp.bfloat16)
        return (total + jnp.dot(first.astype(jnp.float32), right_k.astype(jnp.float32), preferred_element_type=jnp.float32), None)
    total, _ = lax.scan(add_term, jnp.zeros(y.shape, jnp.float32), (left, right))
    shifted = y.astype(jnp.float32) - TAU * total
    if previous is not None:
        shifted = shifted - MOMENTUM * previous.astype(jnp.float32)
    squares = jnp.sum(shifted * shifted)
    return (shifted * (D * lax.rsqrt(squares + EPS))).astype(jnp.bfloat16)

def truncate(y, omega, rank):
    sketch = jnp.dot(y.astype(jnp.float32), omega.astype(jnp.float32), preferred_element_type=jnp.float32)
    gram = jnp.dot(sketch.T, sketch, precision=lax.Precision.HIGHEST)
    factor = jnp.linalg.cholesky(gram)
    keep = (jnp.arange(P_SIZE) < rank).astype(jnp.float32)
    basis = lax.linalg.triangular_solve(factor, sketch.T, left_side=True, lower=True).T * keep[None, :]
    coeffs = jnp.dot(basis.T, y.astype(jnp.float32), precision=lax.Precision.HIGHEST)
    return jnp.dot(basis, coeffs, precision=lax.Precision.HIGHEST).astype(jnp.bfloat16)

def half_sweep(merged, left, right, omega, ranks):

    def single(items):
        y, left_one, right_one, omega_one, rank = items
        previous = None
        for step in range(ITERS):
            y, previous = (gradient_step(y, previous, left_one, right_one), y)
        return truncate(y, omega_one, rank)
    return lax.map(single, (merged, left, right, omega, ranks))

def reference(state, left_env, right_env, inv_singular, sketch_cols, kept_ranks):
    empty = jnp.zeros_like(state[:1])
    from_left = jnp.concatenate([empty, state[:-1]], 0)
    merged = (state.astype(jnp.float32) + from_left.astype(jnp.float32) * inv_singular[:, None, :]).astype(jnp.bfloat16)
    middle = half_sweep(merged, left_env, right_env, sketch_cols[:, 0], kept_ranks)

    def message(items):
        left_one, x_one = items
        x_float = x_one.astype(jnp.float32)
        expanded = jnp.einsum('kij,jn->kin', left_one.astype(jnp.float32), x_float).astype(jnp.bfloat16)
        product = jnp.einsum('ia,kin->kan', x_float, expanded.astype(jnp.float32))
        return (product * (1.0 / D)).astype(jnp.bfloat16)
    messages = lax.map(message, (left_env, middle))
    shifted = jnp.concatenate([jnp.zeros_like(messages[:1]), messages[:-1]], 0)
    left_next = (left_env.astype(jnp.float32) + shifted.astype(jnp.float32)).astype(jnp.bfloat16)
    from_right = jnp.concatenate([middle[1:], empty], 0)
    merged_two = (middle.astype(jnp.float32) + from_right.astype(jnp.float32) * inv_singular[:, None, :]).astype(jnp.bfloat16)
    return half_sweep(merged_two, left_next, right_env, sketch_cols[:, 1], kept_ranks)
```

```python
import jax
import jax.numpy as jnp
from jax import lax
from jax.sharding import PartitionSpec as P

TAU = 0.3
MOMENTUM = 0.5
EPS = 1e-06
F32 = jnp.float32
BF16 = jnp.bfloat16
HI = lax.Precision.HIGHEST
AXES = ("seg", "mpo", "sec")


class Places:
    def __init__(self, mesh):
        self.segs = mesh.shape["seg"]
        self.mpo = mesh.shape["mpo"]
        self.secs = mesh.shape["sec"]

    def route(self, block, target):
        pairs = []
        for s in range(self.segs):
            for m in range(self.mpo):
                for c in range(self.secs):
                    t, n, d = target(s, m, c)
                    if 0 <= t < self.segs:
                        here = (s * self.mpo + m) * self.secs + c
                        pairs.append((here, (t * self.mpo + n) * self.secs + d))
        return lax.ppermute(block, AXES, pairs)

    def core(self, block):
        return self.route(block, lambda s, m, c: (s, m ^ 1, c))

    def side(self, block):
        return self.route(block, lambda s, m, c: (s, m ^ 2, c))

    def shift(self, block, distance):
        return self.route(block, lambda s, m, c: (s + distance, m, c))

    def sec(self, block):
        return self.route(block, lambda s, m, c: (s, m, c ^ 1))

    def diagonal(self, block):
        return self.route(block, lambda s, m, c: (s, m ^ 2, c ^ 1))

    def sec_sum(self, block):
        if self.secs == 2:
            return block + self.sec(block)
        return lax.psum(block, "sec")

    def gather(self, block):
        m = lax.axis_index("mpo")
        side, core = m // 2, m % 2
        c = lax.axis_index("sec")
        height, width = block.shape
        if self.secs == 2:
            pieces = {(0, 0): block, (0, 1): self.side(block), (1, 0): self.sec(block), (1, 1): self.diagonal(block)}
            whole = jnp.zeros((2, 2, 2, height, width), block.dtype)
            for (dc, dx), piece in pieces.items():
                for dk, part in ((0, piece), (1, self.core(piece))):
                    whole = lax.dynamic_update_slice(whole, part[None, None, None], (c ^ dc, core ^ dk, side ^ dx, 0, 0))
        else:
            column = lax.all_gather(block, "sec", axis=0, tiled=False)
            whole = jnp.zeros((self.secs, 2, 2, height, width), block.dtype)
            for dx, piece in ((0, column), (1, self.side(column))):
                for dk, part in ((0, piece), (1, self.core(piece))):
                    whole = lax.dynamic_update_slice(whole, part[:, None, None], (0, core ^ dk, side ^ dx, 0, 0))
        return whole.reshape(-1, width)


def matmul(a, b):
    return jnp.dot(a, b, preferred_element_type=F32)


def products(lefts, rights, full):
    total = 0.0
    for left, right in zip(lefts, rights):
        first = jnp.einsum("kij,jn->kin", left, full, preferred_element_type=F32).astype(BF16)
        total = total + jnp.einsum("kij,kjn->in", first, right, preferred_element_type=F32)
    return total


def scale_of(full, width):
    big = full.astype(F32)
    return width * lax.rsqrt(jnp.sum(big * big) + EPS)


def half_sweep(places, own, lefts, rights, side):
    height, width = own.shape
    full = places.gather(own)
    scale = None
    previous = None
    for step in range(2):
        partial = products(lefts, rights, full)
        mine = lax.dynamic_slice(partial, (side * height, 0), (height, width))
        other = lax.dynamic_slice(partial, ((1 - side) * height, 0), (height, width))
        total = mine + places.side(other.astype(BF16)).astype(F32)
        shifted = own.astype(F32) - TAU * total
        if previous is not None:
            shifted = scale * shifted - MOMENTUM * previous.astype(F32)
        own, previous = shifted.astype(BF16), own
        full = places.gather(own)
        scale = scale_of(full, width)
    return full, scale


def factors(full, scale, omega, rank):
    columns = omega.shape[1]
    keep = (jnp.arange(columns) < rank).astype(F32)
    sketch = matmul(full, omega)
    gram = jnp.dot(sketch.T, sketch, precision=HI)
    cross = jnp.dot(sketch.T, full.astype(F32), precision=HI)
    factor = jnp.linalg.cholesky(gram)
    inverse = lax.linalg.triangular_solve(factor, jnp.eye(columns, dtype=F32), left_side=True, lower=True) * keep[:, None]
    basis = jnp.dot(sketch, inverse.T, precision=HI)
    coeffs = jnp.dot(inverse, cross, precision=HI) * scale
    return basis, coeffs


def on_device(places, state, left_env, right_env, inv_singular, sketch_cols, kept_ranks):
    rows = state[0]
    left = left_env[0]
    right = right_env[0]
    scales = inv_singular[0][None, :]
    rank = kept_ranks[0]
    width = rows.shape[1]
    terms = left.shape[0]
    m = lax.axis_index("mpo")
    side, core = m // 2, m % 2
    c = lax.axis_index("sec")
    half = rows.shape[0] // 2
    height = half // 2
    at = core * half + side * height

    own = lax.dynamic_slice(rows, (at, 0), (height, width))
    behind = places.shift(own, 1)
    merged = (own.astype(F32) + behind.astype(F32) * scales).astype(BF16)
    left_kept = lax.dynamic_slice(left, (0, core * half, 0), (terms, half, width))
    left_given = lax.dynamic_slice(left, (0, (1 - core) * half, 0), (terms, half, width))
    lefts = [left_kept, places.core(left_given)]
    rights = [right, places.core(right)]

    full, scale = half_sweep(places, merged, lefts, rights, side)
    basis, coeffs = factors(full, scale, sketch_cols[0, 0], rank)
    basis = basis.astype(BF16)
    coeffs = coeffs.astype(BF16)
    start = c * (2 * half) + core * half
    basis_half = lax.dynamic_slice(basis, (start, 0), (half, basis.shape[1]))
    basis_own = lax.dynamic_slice(basis, (start + side * height, 0), (height, basis.shape[1]))

    middle = matmul(basis_own, coeffs).astype(BF16)
    ahead = places.shift(middle, -1)
    merged = (middle.astype(F32) + ahead.astype(F32) * scales).astype(BF16)

    def core_matrix(left_part):
        expanded = jnp.einsum("kij,jn->kin", left_part, basis, preferred_element_type=F32).astype(BF16)
        return jnp.einsum("ia,kin->kan", basis_half, expanded, preferred_element_type=F32)

    small = core_matrix(lefts[0]) + places.core(core_matrix(lefts[1]).astype(BF16)).astype(F32)
    small = places.sec_sum(small.astype(BF16))
    small_in = places.shift(small, 1)
    coeffs_in = places.shift(coeffs, 1)
    coeffs_rows = lax.dynamic_slice(coeffs_in, (0, start), (coeffs_in.shape[0], half))

    def next_left(left_part, small_part):
        spread = jnp.einsum("kab,bn->kan", small_part, coeffs_in, preferred_element_type=F32).astype(BF16)
        message = jnp.einsum("ai,kan->kin", coeffs_rows, spread, preferred_element_type=F32)
        message = (message * (1.0 / width)).astype(BF16)
        return (left_part.astype(F32) + message.astype(F32)).astype(BF16)

    lefts = [next_left(lefts[0], small_in), next_left(lefts[1], places.core(small_in))]
    full, scale = half_sweep(places, merged, lefts, rights, side)
    basis, coeffs = factors(full, scale, sketch_cols[0, 1], rank)
    basis_rows = lax.dynamic_slice(basis, (c * 2 * half, 0), (2 * half, basis.shape[1]))
    final_rows = jnp.dot(basis_rows, coeffs, precision=HI).astype(BF16)
    return final_rows[None]


def solution(mesh):
    places = Places(mesh)

    def run(*arrays):
        return on_device(places, *arrays)

    return jax.shard_map(
        run,
        mesh=mesh,
        in_specs=(
            P("seg", "sec", None),
            P("seg", "mpo", "sec", None),
            P("seg", "mpo", None, None),
            P("seg", None),
            P("seg", None, None, None),
            P("seg"),
        ),
        out_specs=P("seg", "sec", None),
        check_vma=False,
    )
```

```python
import functools

import jax
import jax.numpy as jnp
from jax import lax
from jax.experimental import pallas as pl
from jax.experimental.pallas import tpu as pltpu
from jax.sharding import PartitionSpec as P

TAU = 0.3
MOMENTUM = 0.5
EPS = 1e-06
F32 = jnp.float32
BF16 = jnp.bfloat16
AXES = ("seg", "mpo", "sec")


class Places:
    def __init__(self, mesh):
        self.segs = mesh.shape["seg"]
        self.mpo = mesh.shape["mpo"]
        self.secs = mesh.shape["sec"]

    def route(self, block, target):
        pairs = []
        for s in range(self.segs):
            for m in range(self.mpo):
                for c in range(self.secs):
                    t, n, d = target(s, m, c)
                    if 0 <= t < self.segs:
                        here = (s * self.mpo + m) * self.secs + c
                        pairs.append((here, (t * self.mpo + n) * self.secs + d))
        return lax.ppermute(block, AXES, pairs)

    def core(self, block):
        return self.route(block, lambda s, m, c: (s, m ^ 1, c))

    def side(self, block):
        return self.route(block, lambda s, m, c: (s, m ^ 2, c))

    def shift(self, block, distance):
        return self.route(block, lambda s, m, c: (s + distance, m, c))

    def sec(self, block):
        return self.route(block, lambda s, m, c: (s, m, c ^ 1))

    def diagonal(self, block):
        return self.route(block, lambda s, m, c: (s, m ^ 2, c ^ 1))

    def sec_sum(self, block):
        if self.secs == 2:
            return block + self.sec(block)
        return lax.psum(block, "sec")

    def gather(self, block):
        m = lax.axis_index("mpo")
        side, core = m // 2, m % 2
        c = lax.axis_index("sec")
        height, width = block.shape
        if self.secs == 2:
            sent = [(0, 0, block), (0, 1, self.side(block)), (1, 0, self.sec(block)), (1, 1, self.diagonal(block))]
            pieces, offsets = [], []
            for dc, dx, piece in sent:
                for dk, part in ((0, piece), (1, self.core(piece))):
                    pieces.append(part)
                    offsets.append((((c ^ dc) * 2 + (core ^ dk)) * 2 + (side ^ dx)) * height)
            return pieces, offsets
        column = lax.all_gather(block, "sec", axis=0, tiled=False)
        whole = jnp.zeros((self.secs, 2, 2, height, width), block.dtype)
        for dx, piece in ((0, column), (1, self.side(column))):
            for dk, part in ((0, piece), (1, self.core(piece))):
                whole = lax.dynamic_update_slice(whole, part[:, None, None], (0, core ^ dk, side ^ dx, 0, 0))
        return [whole.reshape(-1, width)], [jnp.int32(0)]


def matmul(a, b):
    return jnp.dot(a, b, preferred_element_type=F32)


def exact(a, b, contract):
    return lax.dot_general(a, b, (contract, ((), ())), precision=lax.Precision.HIGHEST, preferred_element_type=F32)


def tree(terms):
    while len(terms) > 1:
        paired = [terms[i] + terms[i + 1] for i in range(0, len(terms) - 1, 2)]
        terms = paired + terms[len(paired) * 2 :]
    return terms[0]


def place(offsets, pieces, y_ref):
    squares = None
    for i, piece in enumerate(pieces):
        height = piece.shape[0]
        at = pl.multiple_of(offsets[i], height) if height < y_ref.shape[0] else 0
        y_ref[pl.ds(at, height), :] = piece[...]
    for r in range(0, y_ref.shape[0], 128):
        big = y_ref[r : r + 128, :].astype(F32)
        part = jnp.sum(big * big, axis=0, keepdims=True)
        squares = part if squares is None else squares + part
    return y_ref.shape[1] * lax.rsqrt(jnp.sum(squares, axis=1, keepdims=True) + EPS)


def step_kernel(count, offsets, *refs):
    pieces = refs[:count]
    left_a, left_b, right_a, right_b, mine, other, scale, y_ref, first, sums = refs[count:]
    width = y_ref.shape[1]
    half = sums.shape[0]
    height = mine.shape[0]
    terms = left_a.shape[0] // half
    scale[...] = jnp.broadcast_to(place(offsets, pieces, y_ref), scale.shape)
    chunk = 512

    def forward(n, carry):
        cols = pl.ds(pl.multiple_of(n * chunk, chunk), chunk)
        for i, left in enumerate((left_a, left_b)):
            value = matmul(left[...], y_ref[:, cols]).astype(BF16)
            for k in range(terms):
                to = pl.multiple_of((i * terms + k) * width + n * chunk, chunk)
                first[:, pl.ds(to, chunk)] = value[k * half : (k + 1) * half]
        return carry

    lax.fori_loop(0, width // chunk, forward, 0)
    depth = terms * width

    def back(n, carry):
        cols = pl.ds(pl.multiple_of(n * chunk, chunk), chunk)
        sums[:, cols] = matmul(first[:, :depth], right_a[:, cols]) + matmul(first[:, depth:], right_b[:, cols])
        return carry

    lax.fori_loop(0, width // chunk, back, 0)
    side = offsets[count]
    mine[...] = sums[pl.ds(pl.multiple_of(side * height, height), height), :]
    other[...] = sums[pl.ds(pl.multiple_of((1 - side) * height, height), height), :].astype(BF16)


VMEM = pl.BlockSpec(memory_space=pltpu.VMEM)
SMEM = pl.BlockSpec(memory_space=pltpu.SMEM)


def products(pieces, offsets, side, lefts, rights):
    width = pieces[0].shape[1]
    terms, half = lefts[0].shape[:2]
    height = half // 2
    count = len(pieces)
    scalars = jnp.stack(offsets + [side]).astype(jnp.int32)
    flat = [a.reshape(-1, width) for a in list(lefts) + list(rights)]
    return pl.pallas_call(
        functools.partial(step_kernel, count),
        out_shape=(
            jax.ShapeDtypeStruct((height, width), F32),
            jax.ShapeDtypeStruct((height, width), BF16),
            jax.ShapeDtypeStruct((8, 128), F32),
        ),
        in_specs=[SMEM] + [VMEM] * (count + 4),
        out_specs=(VMEM, VMEM, VMEM),
        scratch_shapes=[
            pltpu.VMEM((width, width), BF16),
            pltpu.VMEM((half, 2 * terms * width), BF16),
            pltpu.VMEM((half, width), F32),
        ],
        compiler_params=pltpu.CompilerParams(vmem_limit_bytes=28 << 20),
    )(scalars, *pieces, *flat)


def small_inverse(entries, size):
    a = dict(entries)

    def get(i, j):
        return a[(i, j)] if i >= j else a[(j, i)]

    for p in range(0, size, 2):
        q = p + 1
        x, y, z = get(p, p), get(q, p), get(q, q)
        d = 1.0 / (x * z - y * y)
        xx, xy, yy = z * d, -(y * d), x * d
        rest = [i for i in range(size) if i not in (p, q)]
        old = {i: (get(i, p), get(i, q)) for i in rest}
        new = {i: (old[i][0] * xx + old[i][1] * xy, old[i][0] * xy + old[i][1] * yy) for i in rest}
        for n, i in enumerate(rest):
            for j in rest[: n + 1]:
                a[(i, j)] = a[(i, j)] - (new[i][0] * old[j][0] + new[i][1] * old[j][1])
        for i in rest:
            for k, j in ((0, p), (1, q)):
                a[(max(i, j), min(i, j))] = new[i][k]
        a[(p, p)], a[(q, p)], a[(q, q)] = -xx, -xy, -yy
    return {k: -v for k, v in a.items()}


def eliminate(m_ref, x_ref, y_ref, s_ref):
    size = m_ref.shape[0]
    lanes = lax.broadcasted_iota(jnp.int32, (8, size), 1)
    subs = lax.broadcasted_iota(jnp.int32, (8, size), 0)
    for b in range(size // 8):
        at = 8 * b
        base = (b % 2) * 64
        rows = m_ref[at : at + 8, :]
        for j in range(8):
            s_ref[base + 8 * j : base + 8 * j + 8, :] = jnp.broadcast_to(rows[:, at + j : at + j + 1], (8, 128))
        entries = {}
        for j in range(8):
            for i in range(j, 8):
                spot = base + 8 * j + i
                entries[(i, j)] = jnp.broadcast_to(s_ref[spot : spot + 1, :], (8, 128))
        inverse = small_inverse(entries, 8)
        inside = (lanes >= at) & (lanes < at + 8)
        rows = jnp.where(inside, (lanes - at == subs).astype(F32), rows)
        m_ref[at : at + 8, :] = rows
        single = [jnp.broadcast_to(m_ref[at + k : at + k + 1, :], (8, size)) for k in range(8)]
        solved = []
        for k in range(8):
            parts = []
            for h in range(0, size, 128):
                parts.append(tree([inverse[(max(k, n), min(k, n))] * single[n][:, h : h + 128] for n in range(8)]))
            solved.append(jnp.concatenate(parts, 1))
        merged = solved[0]
        for k in range(1, 8):
            merged = jnp.where(subs == k, solved[k], merged)
        done = lanes < at + 8
        x_ref[at : at + 8, :] = jnp.where(done, rows, 0.0)
        y_ref[at : at + 8, :] = jnp.where(done, merged, 0.0)
        for g in range(at + 8, size, 8):
            below = m_ref[g : g + 8, :]
            terms = [jnp.broadcast_to(below[:, at + k : at + k + 1], (8, size)) * solved[k] for k in range(8)]
            m_ref[g : g + 8, :] = jnp.where(inside, 0.0, below) - tree(terms)


def truncate_kernel(count, last, scalars, *refs):
    pieces = refs[:count]
    omega = refs[count]
    outs = refs[count + 1 : -9]
    y_ref, s_ref, high, low, cross, m_ref, x_ref, v_ref, spread = refs[-9:]
    width = y_ref.shape[1]
    size = m_ref.shape[0]
    scale = place(scalars, pieces, y_ref)
    at, rank = scalars[count], scalars[count + 1]
    sketch = matmul(y_ref[...], omega[...]) * scale
    s_ref[...] = sketch
    tall_high = sketch.astype(BF16)
    tall_low = (sketch - tall_high.astype(F32)).astype(BF16)
    turned = sketch.T
    high[...] = turned.astype(BF16)
    low[...] = (turned - high[...].astype(F32)).astype(BF16)
    gram = matmul(high[...], tall_high) + matmul(high[...], tall_low) + matmul(low[...], tall_high)
    row = lax.broadcasted_iota(jnp.int32, (size, size), 0)
    col = lax.broadcasted_iota(jnp.int32, (size, size), 1)
    m_ref[...] = jnp.where((row < rank) & (col < rank), gram, (row == col).astype(F32))
    cross[...] = (matmul(high[...], y_ref[...]) + matmul(low[...], y_ref[...])) * scale
    eliminate(m_ref, x_ref, v_ref, spread)
    kept = lax.broadcasted_iota(jnp.int32, (size, width), 0) < rank
    coeffs = jnp.where(kept, exact(v_ref[...], cross[...], ((1,), (0,))), 0.0)
    if last:
        result = outs[0]
        rows = result.shape[0]
        basis = exact(s_ref[pl.ds(pl.multiple_of(at, rows), rows), :], x_ref[...], ((1,), (1,)))
        result[...] = exact(basis, coeffs, ((1,), (0,))).astype(BF16)
    else:
        middle, basis, coeffs_out = outs
        rows = middle.shape[0]
        coeffs_out[...] = coeffs.astype(BF16)
        basis[...] = exact(s_ref[...], x_ref[...], ((1,), (1,))).astype(BF16)
        middle[...] = matmul(basis[pl.ds(pl.multiple_of(at, rows), rows), :], coeffs_out[...]).astype(BF16)


def truncate(pieces, offsets, at, rank, omega, rows, last):
    width = pieces[0].shape[1]
    size = omega.shape[1]
    count = len(pieces)
    scalars = jnp.stack(offsets + [at, rank]).astype(jnp.int32)
    shapes = [jax.ShapeDtypeStruct((rows, width), BF16)]
    if not last:
        shapes += [jax.ShapeDtypeStruct((width, size), BF16), jax.ShapeDtypeStruct((size, width), BF16)]
    return pl.pallas_call(
        functools.partial(truncate_kernel, count, last),
        out_shape=tuple(shapes),
        in_specs=[SMEM] + [VMEM] * (count + 1),
        out_specs=tuple([VMEM] * len(shapes)),
        scratch_shapes=[
            pltpu.VMEM((width, width), BF16),
            pltpu.VMEM((width, size), F32),
            pltpu.VMEM((size, width), BF16),
            pltpu.VMEM((size, width), BF16),
            pltpu.VMEM((size, width), F32),
            pltpu.VMEM((size, size), F32),
            pltpu.VMEM((size, size), F32),
            pltpu.VMEM((size, size), F32),
            pltpu.VMEM((128, 128), F32),
        ],
        compiler_params=pltpu.CompilerParams(vmem_limit_bytes=24 << 20),
    )(scalars, *pieces, omega)


def half_sweep(places, own, lefts, rights, side):
    pieces, offsets = places.gather(own)
    previous = None
    for step in range(2):
        mine, other, scale = products(pieces, offsets, side, lefts, rights)
        total = mine + places.side(other).astype(F32)
        shifted = own.astype(F32) - TAU * total
        if previous is not None:
            shifted = scale[:1, :1] * shifted - MOMENTUM * previous.astype(F32)
        own, previous = shifted.astype(BF16), own
        pieces, offsets = places.gather(own)
    return pieces, offsets


def on_device(places, state, left_env, right_env, inv_singular, sketch_cols, kept_ranks):
    rows = state[0]
    left = left_env[0]
    right = right_env[0]
    scales = inv_singular[0][None, :]
    rank = kept_ranks[0]
    width = rows.shape[1]
    terms = left.shape[0]
    m = lax.axis_index("mpo")
    side, core = m // 2, m % 2
    c = lax.axis_index("sec")
    half = rows.shape[0] // 2
    height = half // 2
    at = core * half + side * height

    own = lax.dynamic_slice(rows, (at, 0), (height, width))
    behind = places.shift(own, 1)
    merged = (own.astype(F32) + behind.astype(F32) * scales).astype(BF16)
    left_kept = lax.dynamic_slice(left, (0, core * half, 0), (terms, half, width))
    left_given = lax.dynamic_slice(left, (0, (1 - core) * half, 0), (terms, half, width))
    lefts = [left_kept, places.core(left_given)]
    rights = [right, places.core(right)]

    start = c * (2 * half) + core * half
    pieces, offsets = half_sweep(places, merged, lefts, rights, side)
    middle, basis, coeffs = truncate(pieces, offsets, start + side * height, rank, sketch_cols[0, 0], height, False)
    basis_half = lax.dynamic_slice(basis, (start, 0), (half, basis.shape[1]))
    ahead = places.shift(middle, -1)
    merged = (middle.astype(F32) + ahead.astype(F32) * scales).astype(BF16)

    def core_matrix(left_part):
        expanded = jnp.einsum("kij,jn->kin", left_part, basis, preferred_element_type=F32).astype(BF16)
        return jnp.einsum("ia,kin->kan", basis_half, expanded, preferred_element_type=F32)

    small = core_matrix(lefts[0]) + places.core(core_matrix(lefts[1]).astype(BF16)).astype(F32)
    small = places.sec_sum(small.astype(BF16))
    small_in = places.shift(small, 1)
    coeffs_in = places.shift(coeffs, 1)
    coeffs_rows = lax.dynamic_slice(coeffs_in, (0, start), (coeffs_in.shape[0], half))

    def next_left(left_part, small_part):
        spread = jnp.einsum("kab,bn->kan", small_part, coeffs_in, preferred_element_type=F32).astype(BF16)
        message = jnp.einsum("ai,kan->kin", coeffs_rows, spread, preferred_element_type=F32)
        message = (message * (1.0 / width)).astype(BF16)
        return (left_part.astype(F32) + message.astype(F32)).astype(BF16)

    lefts = [next_left(lefts[0], small_in), next_left(lefts[1], places.core(small_in))]
    pieces, offsets = half_sweep(places, merged, lefts, rights, side)
    (final_rows,) = truncate(pieces, offsets, c * (2 * half), rank, sketch_cols[0, 1], 2 * half, True)
    return final_rows[None]


def solution(mesh):
    places = Places(mesh)

    def run(*arrays):
        return on_device(places, *arrays)

    return jax.shard_map(
        run,
        mesh=mesh,
        in_specs=(
            P("seg", "sec", None),
            P("seg", "mpo", "sec", None),
            P("seg", "mpo", None, None),
            P("seg", None),
            P("seg", None, None, None),
            P("seg"),
        ),
        out_specs=P("seg", "sec", None),
        check_vma=False,
    )
```

```python
import functools

import jax
import jax.numpy as jnp
from jax import lax
from jax.experimental import pallas as pl
from jax.experimental.pallas import tpu as pltpu
from jax.sharding import PartitionSpec as P

TAU = 0.3
MOMENTUM = 0.5
EPS = 1e-06
F32 = jnp.float32
BF16 = jnp.bfloat16
AXES = ("seg", "mpo", "sec")


class Places:
    def __init__(self, mesh):
        self.segs = mesh.shape["seg"]
        self.mpo = mesh.shape["mpo"]
        self.secs = mesh.shape["sec"]

    def route(self, block, target):
        pairs = []
        for s in range(self.segs):
            for m in range(self.mpo):
                for c in range(self.secs):
                    t, n, d = target(s, m, c)
                    if 0 <= t < self.segs:
                        here = (s * self.mpo + m) * self.secs + c
                        pairs.append((here, (t * self.mpo + n) * self.secs + d))
        return lax.ppermute(block, AXES, pairs)

    def core(self, block):
        return self.route(block, lambda s, m, c: (s, m ^ 1, c))

    def side(self, block):
        return self.route(block, lambda s, m, c: (s, m ^ 2, c))

    def shift(self, block, distance):
        return self.route(block, lambda s, m, c: (s + distance, m, c))

    def sec(self, block):
        return self.route(block, lambda s, m, c: (s, m, c ^ 1))

    def diagonal(self, block):
        return self.route(block, lambda s, m, c: (s, m ^ 2, c ^ 1))

    def sec_sum(self, block):
        if self.secs == 2:
            return block + self.sec(block)
        return lax.psum(block, "sec")

    def gather(self, block):
        m = lax.axis_index("mpo")
        side, core = m // 2, m % 2
        c = lax.axis_index("sec")
        height, width = block.shape
        if self.secs == 2:
            sent = [(0, 0, block), (0, 1, self.side(block)), (1, 0, self.sec(block)), (1, 1, self.diagonal(block))]
            pieces, offsets = [], []
            for dc, dx, piece in sent:
                for dk, part in ((0, piece), (1, self.core(piece))):
                    pieces.append(part)
                    offsets.append((((c ^ dc) * 2 + (core ^ dk)) * 2 + (side ^ dx)) * height)
            return pieces, offsets
        column = lax.all_gather(block, "sec", axis=0, tiled=False)
        whole = jnp.zeros((self.secs, 2, 2, height, width), block.dtype)
        for dx, piece in ((0, column), (1, self.side(column))):
            for dk, part in ((0, piece), (1, self.core(piece))):
                whole = lax.dynamic_update_slice(whole, part[:, None, None], (0, core ^ dk, side ^ dx, 0, 0))
        return [whole.reshape(-1, width)], [jnp.int32(0)]


def matmul(a, b):
    return jnp.dot(a, b, preferred_element_type=F32)


def exact(a, b, contract):
    return lax.dot_general(a, b, (contract, ((), ())), precision=lax.Precision.HIGHEST, preferred_element_type=F32)


def split(a):
    high = a.astype(BF16)
    return high, (a - high.astype(F32)).astype(BF16)


def close(a, b):
    a_high, a_low = split(a)
    b_high, b_low = split(b)
    return matmul(a_high, b_high) + matmul(a_high, b_low) + matmul(a_low, b_high)


def tree(terms):
    while len(terms) > 1:
        paired = [terms[i] + terms[i + 1] for i in range(0, len(terms) - 1, 2)]
        terms = paired + terms[len(paired) * 2 :]
    return terms[0]


def place(offsets, pieces, y_ref):
    squares = None
    for i, piece in enumerate(pieces):
        height = piece.shape[0]
        at = pl.multiple_of(offsets[i], height) if height < y_ref.shape[0] else 0
        y_ref[pl.ds(at, height), :] = piece[...]
    for r in range(0, y_ref.shape[0], 128):
        big = y_ref[r : r + 128, :].astype(F32)
        part = jnp.sum(big * big, axis=0, keepdims=True)
        squares = part if squares is None else squares + part
    return y_ref.shape[1] * lax.rsqrt(jnp.sum(squares, axis=1, keepdims=True) + EPS)


def step_kernel(count, offsets, *refs):
    pieces = refs[:count]
    left_a, left_b, right_a, right_b, mine, other, scale, y_ref, first, sums, left, right, sems = refs[count:]
    width = y_ref.shape[1]
    half = sums.shape[0]
    height = mine.shape[0]
    tall = left_a.shape[0]
    terms = tall // half
    chunk = width // 2
    depth = terms * width
    left_copies = []
    right_copies = []
    for i, source in enumerate((left_a, left_b)):
        left_copies.append(pltpu.make_async_copy(source, left.at[i], sems.at[i]))
        left_copies[-1].start()
    for n in range(2):
        for i, source in enumerate((right_a, right_b)):
            cols = slice(n * chunk, (n + 1) * chunk)
            copy = pltpu.make_async_copy(source.at[:, cols], right.at[n, i], sems.at[2 + 2 * n + i])
            copy.start()
            right_copies.append(copy)
    scale[...] = jnp.broadcast_to(place(offsets, pieces, y_ref), scale.shape)
    for i in range(2):
        left_copies[i].wait()

        def forward(n, carry):
            cols = pl.ds(pl.multiple_of(n * chunk, chunk), chunk)
            value = matmul(left[i], y_ref[:, cols]).astype(BF16)
            for k in range(terms):
                to = pl.multiple_of((i * terms + k) * width + n * chunk, chunk)
                first[:, pl.ds(to, chunk)] = value[k * half : (k + 1) * half]
            return carry

        lax.fori_loop(0, 2, forward, 0)
    for n in range(2):
        right_copies[2 * n].wait()
        right_copies[2 * n + 1].wait()
        cols = slice(n * chunk, (n + 1) * chunk)
        sums[:, cols] = matmul(first[:, :depth], right[n, 0]) + matmul(first[:, depth:], right[n, 1])
    side = offsets[count]
    mine[...] = sums[pl.ds(pl.multiple_of(side * height, height), height), :]
    other[...] = sums[pl.ds(pl.multiple_of((1 - side) * height, height), height), :].astype(BF16)


STEP_VMEM = 28 << 20
CUT_VMEM = 28 << 20
ANY = pl.BlockSpec(memory_space=pl.ANY)
VMEM = pl.BlockSpec(memory_space=pltpu.VMEM)
SMEM = pl.BlockSpec(memory_space=pltpu.SMEM)


def products(pieces, offsets, side, lefts, rights):
    width = pieces[0].shape[1]
    terms, half = lefts[0].shape[:2]
    height = half // 2
    count = len(pieces)
    scalars = jnp.stack(offsets + [side]).astype(jnp.int32)
    flat = [a.reshape(-1, width) for a in list(lefts) + list(rights)]
    return pl.pallas_call(
        functools.partial(step_kernel, count),
        out_shape=(
            jax.ShapeDtypeStruct((height, width), F32),
            jax.ShapeDtypeStruct((height, width), BF16),
            jax.ShapeDtypeStruct((8, 128), F32),
        ),
        in_specs=[SMEM] + [VMEM] * count + [ANY] * 4,
        out_specs=(VMEM, VMEM, VMEM),
        scratch_shapes=[
            pltpu.VMEM((width, width), BF16),
            pltpu.VMEM((half, 2 * terms * width), BF16),
            pltpu.VMEM((half, width), F32),
            pltpu.VMEM((2, terms * half, width), BF16),
            pltpu.VMEM((2, 2, terms * width, width // 2), BF16),
            pltpu.SemaphoreType.DMA((6,)),
        ],
        compiler_params=pltpu.CompilerParams(vmem_limit_bytes=STEP_VMEM),
    )(scalars, *pieces, *flat)


def small_inverse(entries, size):
    a = dict(entries)

    def get(i, j):
        return a[(i, j)] if i >= j else a[(j, i)]

    for p in range(0, size, 2):
        q = p + 1
        x, y, z = get(p, p), get(q, p), get(q, q)
        d = 1.0 / (x * z - y * y)
        xx, xy, yy = z * d, -(y * d), x * d
        rest = [i for i in range(size) if i not in (p, q)]
        old = {i: (get(i, p), get(i, q)) for i in rest}
        new = {i: (old[i][0] * xx + old[i][1] * xy, old[i][0] * xy + old[i][1] * yy) for i in rest}
        for n, i in enumerate(rest):
            for j in rest[: n + 1]:
                a[(i, j)] = a[(i, j)] - (new[i][0] * old[j][0] + new[i][1] * old[j][1])
        for i in rest:
            for k, j in ((0, p), (1, q)):
                a[(max(i, j), min(i, j))] = new[i][k]
        a[(p, p)], a[(q, p)], a[(q, q)] = -xx, -xy, -yy
    return {k: -v for k, v in a.items()}


def eliminate(m_ref, x_ref, y_ref, s_ref):
    size = m_ref.shape[0]
    lanes = lax.broadcasted_iota(jnp.int32, (8, size), 1)
    subs = lax.broadcasted_iota(jnp.int32, (8, size), 0)
    for b in range(size // 8):
        at = 8 * b
        base = (b % 2) * 64
        rows = m_ref[at : at + 8, :]
        for j in range(8):
            s_ref[base + 8 * j : base + 8 * j + 8, :] = jnp.broadcast_to(rows[:, at + j : at + j + 1], (8, 128))
        entries = {}
        for j in range(8):
            for i in range(j, 8):
                spot = base + 8 * j + i
                entries[(i, j)] = jnp.broadcast_to(s_ref[spot : spot + 1, :], (8, 128))
        inverse = small_inverse(entries, 8)
        inside = (lanes >= at) & (lanes < at + 8)
        rows = jnp.where(inside, (lanes - at == subs).astype(F32), rows)
        m_ref[at : at + 8, :] = rows
        single = [jnp.broadcast_to(m_ref[at + k : at + k + 1, :], (8, size)) for k in range(8)]
        solved = []
        for k in range(8):
            parts = []
            for h in range(0, size, 128):
                parts.append(tree([inverse[(max(k, n), min(k, n))] * single[n][:, h : h + 128] for n in range(8)]))
            solved.append(jnp.concatenate(parts, 1))
        merged = solved[0]
        for k in range(1, 8):
            merged = jnp.where(subs == k, solved[k], merged)
        done = lanes < at + 8
        x_ref[at : at + 8, :] = jnp.where(done, rows, 0.0)
        y_ref[at : at + 8, :] = jnp.where(done, merged, 0.0)
        for g in range(at + 8, size, 8):
            below = m_ref[g : g + 8, :]
            terms = [jnp.broadcast_to(below[:, at + k : at + k + 1], (8, size)) * solved[k] for k in range(8)]
            m_ref[g : g + 8, :] = jnp.where(inside, 0.0, below) - tree(terms)


def truncate_kernel(count, last, scalars, *refs):
    pieces = refs[:count]
    omega = refs[count]
    lefts = () if last else refs[count + 1 : count + 3]
    outs = refs[count + 1 + len(lefts) : -9]
    y_ref, s_ref, high, low, cross, m_ref, x_ref, v_ref, spread = refs[-9:]
    width = y_ref.shape[1]
    size = m_ref.shape[0]
    scale = place(scalars, pieces, y_ref)
    at, rank = scalars[count], scalars[count + 1]
    sketch = matmul(y_ref[...], omega[...]) * scale
    s_ref[...] = sketch
    tall_high = sketch.astype(BF16)
    tall_low = (sketch - tall_high.astype(F32)).astype(BF16)
    turned = sketch.T
    high[...] = turned.astype(BF16)
    low[...] = (turned - high[...].astype(F32)).astype(BF16)
    gram = matmul(high[...], tall_high) + matmul(high[...], tall_low) + matmul(low[...], tall_high)
    row = lax.broadcasted_iota(jnp.int32, (size, size), 0)
    col = lax.broadcasted_iota(jnp.int32, (size, size), 1)
    m_ref[...] = jnp.where((row < rank) & (col < rank), gram, (row == col).astype(F32))
    cross[...] = (matmul(high[...], y_ref[...]) + matmul(low[...], y_ref[...])) * scale
    eliminate(m_ref, x_ref, v_ref, spread)
    kept = lax.broadcasted_iota(jnp.int32, (size, width), 0) < rank
    coeffs = jnp.where(kept, exact(v_ref[...], cross[...], ((1,), (0,))), 0.0)
    if last:
        result = outs[0]
        rows = result.shape[0]
        basis = exact(s_ref[pl.ds(pl.multiple_of(at, rows), rows), :], x_ref[...], ((1,), (1,)))
        result[...] = close(basis, coeffs).astype(BF16)
    else:
        middle, coeffs_out, small_a, small_b = outs
        rows = middle.shape[0]
        half = 2 * rows
        coeffs_out[...] = coeffs.astype(BF16)
        basis = exact(s_ref[...], x_ref[...], ((1,), (1,)))
        s_ref[...] = basis
        own = s_ref[pl.ds(pl.multiple_of(at, rows), rows), :].astype(BF16)
        middle[...] = matmul(own, coeffs_out[...]).astype(BF16)
        start = pl.multiple_of(scalars[count + 2], half)
        turned = s_ref[pl.ds(start, half), :].T.astype(BF16)
        basis = basis.astype(BF16)
        for left, small in zip(lefts, (small_a, small_b)):
            expanded = matmul(left[...], basis).astype(BF16)
            for k in range(left.shape[0] // half):
                part = matmul(turned, expanded[k * half : (k + 1) * half])
                small[k * size : (k + 1) * size, :] = part.astype(small.dtype)


def next_kernel(left_a, left_b, small_a, small_b, coeffs, rows, out_a, out_b):
    half = rows.shape[0]
    size, width = coeffs.shape
    for left, small, out in ((left_a, small_a, out_a), (left_b, small_b, out_b)):
        for k in range(left.shape[0] // half):
            part = slice(k * half, (k + 1) * half)
            spread = matmul(small[k * size : (k + 1) * size, :], coeffs[...]).astype(BF16)
            message = (matmul(rows[...], spread) * (1.0 / width)).astype(BF16)
            out[part, :] = (left[part, :].astype(F32) + message.astype(F32)).astype(BF16)


def next_lefts(lefts, smalls, coeffs, rows):
    shape = lefts[0].shape
    flat = [a.reshape(-1, shape[2]) for a in lefts]
    outs = pl.pallas_call(
        next_kernel,
        out_shape=[jax.ShapeDtypeStruct(a.shape, BF16) for a in flat],
        in_specs=[VMEM] * 6,
        out_specs=[VMEM] * 2,
        compiler_params=pltpu.CompilerParams(vmem_limit_bytes=STEP_VMEM),
    )(*flat, *smalls, coeffs, rows)
    return [a.reshape(shape) for a in outs]


def truncate(pieces, offsets, at, rank, omega, rows, lefts=None, start=None):
    width = pieces[0].shape[1]
    size = omega.shape[1]
    count = len(pieces)
    last = lefts is None
    scalars = offsets + [at, rank] + ([] if last else [start])
    scalars = jnp.stack(scalars).astype(jnp.int32)
    shapes = [jax.ShapeDtypeStruct((rows, width), BF16)]
    flat = []
    if not last:
        terms = lefts[0].shape[0]
        shapes += [
            jax.ShapeDtypeStruct((size, width), BF16),
            jax.ShapeDtypeStruct((terms * size, size), F32),
            jax.ShapeDtypeStruct((terms * size, size), BF16),
        ]
        flat = [a.reshape(-1, width) for a in lefts]
    return pl.pallas_call(
        functools.partial(truncate_kernel, count, last),
        out_shape=tuple(shapes),
        in_specs=[SMEM] + [VMEM] * (count + 1 + len(flat)),
        out_specs=tuple([VMEM] * len(shapes)),
        scratch_shapes=[
            pltpu.VMEM((width, width), BF16),
            pltpu.VMEM((width, size), F32),
            pltpu.VMEM((size, width), BF16),
            pltpu.VMEM((size, width), BF16),
            pltpu.VMEM((size, width), F32),
            pltpu.VMEM((size, size), F32),
            pltpu.VMEM((size, size), F32),
            pltpu.VMEM((size, size), F32),
            pltpu.VMEM((128, 128), F32),
        ],
        compiler_params=pltpu.CompilerParams(vmem_limit_bytes=CUT_VMEM),
    )(scalars, *pieces, omega, *flat)


def half_sweep(places, own, lefts, rights, side):
    pieces, offsets = places.gather(own)
    previous = None
    for step in range(2):
        mine, other, scale = products(pieces, offsets, side, lefts, rights)
        total = mine + places.side(other).astype(F32)
        shifted = own.astype(F32) - TAU * total
        if previous is not None:
            shifted = scale[:1, :1] * shifted - MOMENTUM * previous.astype(F32)
        own, previous = shifted.astype(BF16), own
        pieces, offsets = places.gather(own)
    return pieces, offsets


def on_device(places, state, left_env, right_env, inv_singular, sketch_cols, kept_ranks):
    rows = state[0]
    left = left_env[0]
    right = right_env[0]
    scales = inv_singular[0][None, :]
    rank = kept_ranks[0]
    width = rows.shape[1]
    terms = left.shape[0]
    m = lax.axis_index("mpo")
    side, core = m // 2, m % 2
    c = lax.axis_index("sec")
    half = rows.shape[0] // 2
    height = half // 2
    at = core * half + side * height

    own = lax.dynamic_slice(rows, (at, 0), (height, width))
    behind = places.shift(own, 1)
    merged = (own.astype(F32) + behind.astype(F32) * scales).astype(BF16)
    left, merged = lax.optimization_barrier((left, merged))
    left_kept = lax.dynamic_slice(left, (0, core * half, 0), (terms, half, width))
    left_given = lax.dynamic_slice(left, (0, (1 - core) * half, 0), (terms, half, width))
    lefts = [left_kept, places.core(left_given)]
    rights = [right, places.core(right)]

    start = c * (2 * half) + core * half
    pieces, offsets = half_sweep(places, merged, lefts, rights, side)
    middle, coeffs, small_a, small_b = truncate(
        pieces, offsets, start + side * height, rank, sketch_cols[0, 0], height, lefts, start
    )
    size = coeffs.shape[0]
    ahead = places.shift(middle, -1)
    small = small_a + places.core(small_b).astype(F32)
    small = places.sec_sum(small.astype(BF16))
    coeffs_in = places.shift(lax.dynamic_slice(coeffs, (core * (size // 2), 0), (size // 2, width)), 1)
    coeffs_pair = places.core(coeffs_in)
    coeffs_in = jnp.where(core == 0, jnp.concatenate([coeffs_in, coeffs_pair]), jnp.concatenate([coeffs_pair, coeffs_in]))
    coeffs_rows = lax.dynamic_slice(coeffs_in, (0, start), (size, half)).T
    merged = (middle.astype(F32) + ahead.astype(F32) * scales).astype(BF16)
    small_in = places.shift(small, 1)
    lefts = next_lefts(lefts, [small_in, places.core(small_in)], coeffs_in, coeffs_rows)
    pieces, offsets = half_sweep(places, merged, lefts, rights, side)
    (final_rows,) = truncate(pieces, offsets, c * (2 * half), rank, sketch_cols[0, 1], 2 * half)
    return final_rows[None]


def solution(mesh):
    places = Places(mesh)

    def run(*arrays):
        return on_device(places, *arrays)

    return jax.shard_map(
        run,
        mesh=mesh,
        in_specs=(
            P("seg", "sec", None),
            P("seg", "mpo", "sec", None),
            P("seg", "mpo", None, None),
            P("seg", None),
            P("seg", None, None, None),
            P("seg"),
        ),
        out_specs=P("seg", "sec", None),
        check_vma=False,
    )
```

```python
import functools

import jax
import jax.numpy as jnp
from jax import lax
from jax.experimental import pallas as pl
from jax.experimental.pallas import tpu as pltpu
from jax.sharding import PartitionSpec as P

TAU = 0.3
MOMENTUM = 0.5
EPS = 1e-06
F32 = jnp.float32
BF16 = jnp.bfloat16
AXES = ("seg", "mpo", "sec")


class Places:
    def __init__(self, mesh):
        self.segs = mesh.shape["seg"]
        self.mpo = mesh.shape["mpo"]
        self.secs = mesh.shape["sec"]

    def route(self, block, target):
        pairs = []
        for s in range(self.segs):
            for m in range(self.mpo):
                for c in range(self.secs):
                    t, n, d = target(s, m, c)
                    if 0 <= t < self.segs:
                        here = (s * self.mpo + m) * self.secs + c
                        pairs.append((here, (t * self.mpo + n) * self.secs + d))
        return lax.ppermute(block, AXES, pairs)

    def core(self, block):
        return self.route(block, lambda s, m, c: (s, m ^ 1, c))

    def side(self, block):
        return self.route(block, lambda s, m, c: (s, m ^ 2, c))

    def shift(self, block, distance):
        return self.route(block, lambda s, m, c: (s + distance, m, c))

    def sec(self, block):
        return self.route(block, lambda s, m, c: (s, m, c ^ 1))

    def diagonal(self, block):
        return self.route(block, lambda s, m, c: (s, m ^ 2, c ^ 1))

    def sec_sum(self, block):
        if self.secs == 2:
            return block + self.sec(block)
        return lax.psum(block, "sec")

    def gather(self, block):
        m = lax.axis_index("mpo")
        side, core = m // 2, m % 2
        c = lax.axis_index("sec")
        height, width = block.shape
        if self.secs == 2:
            sent = [(0, 0, block), (0, 1, self.side(block)), (1, 0, self.sec(block)), (1, 1, self.diagonal(block))]
            pieces, offsets = [], []
            for dc, dx, piece in sent:
                for dk, part in ((0, piece), (1, self.core(piece))):
                    pieces.append(part)
                    offsets.append((((c ^ dc) * 2 + (core ^ dk)) * 2 + (side ^ dx)) * height)
            return pieces, offsets
        column = lax.all_gather(block, "sec", axis=0, tiled=False)
        whole = jnp.zeros((self.secs, 2, 2, height, width), block.dtype)
        for dx, piece in ((0, column), (1, self.side(column))):
            for dk, part in ((0, piece), (1, self.core(piece))):
                whole = lax.dynamic_update_slice(whole, part[:, None, None], (0, core ^ dk, side ^ dx, 0, 0))
        return [whole.reshape(-1, width)], [jnp.int32(0)]


def matmul(a, b):
    return jnp.dot(a, b, preferred_element_type=F32)


def exact(a, b, contract):
    return lax.dot_general(a, b, (contract, ((), ())), precision=lax.Precision.HIGHEST, preferred_element_type=F32)


def split(a):
    high = a.astype(BF16)
    return high, (a - high.astype(F32)).astype(BF16)


def close(a, b):
    a_high, a_low = split(a)
    b_high, b_low = split(b)
    return matmul(a_high, b_high) + matmul(a_high, b_low) + matmul(a_low, b_high)


def tree(terms):
    while len(terms) > 1:
        paired = [terms[i] + terms[i + 1] for i in range(0, len(terms) - 1, 2)]
        terms = paired + terms[len(paired) * 2 :]
    return terms[0]


def place(offsets, pieces, y_ref):
    squares = None
    for i, piece in enumerate(pieces):
        height = piece.shape[0]
        at = pl.multiple_of(offsets[i], height) if height < y_ref.shape[0] else 0
        y_ref[pl.ds(at, height), :] = piece[...]
    for r in range(0, y_ref.shape[0], 128):
        big = y_ref[r : r + 128, :].astype(F32)
        part = jnp.sum(big * big, axis=0, keepdims=True)
        squares = part if squares is None else squares + part
    return y_ref.shape[1] * lax.rsqrt(jnp.sum(squares, axis=1, keepdims=True) + EPS)


def step_kernel(count, offsets, *refs):
    pieces = refs[:count]
    left, right, mine, other, scale, y_ref, first, sums = refs[count:]
    width = y_ref.shape[1]
    half = sums.shape[0]
    height = mine.shape[0]
    terms = left.shape[0] // half
    scale[...] = jnp.broadcast_to(place(offsets, pieces, y_ref), scale.shape)
    chunk = width // 2

    def forward(n, carry):
        cols = pl.ds(pl.multiple_of(n * chunk, chunk), chunk)
        for i in range(2):
            part = terms // 2 * half
            value = matmul(left[i * part : (i + 1) * part, :], y_ref[:, cols]).astype(BF16)
            for k in range(terms // 2):
                to = pl.multiple_of((i * (terms // 2) + k) * width + n * chunk, chunk)
                first[:, pl.ds(to, chunk)] = value[k * half : (k + 1) * half]
        return carry

    lax.fori_loop(0, 2, forward, 0)

    def back(n, carry):
        cols = pl.ds(pl.multiple_of(n * chunk, chunk), chunk)
        sums[:, cols] = matmul(first[...], right[:, cols])
        return carry

    lax.fori_loop(0, 2, back, 0)
    side = offsets[count]
    mine[...] = sums[pl.ds(pl.multiple_of(side * height, height), height), :]
    other[...] = sums[pl.ds(pl.multiple_of((1 - side) * height, height), height), :].astype(BF16)


STEP_VMEM = 30 << 20
SMALL_VMEM = 16 << 20
CUT_VMEM = 28 << 20
VMEM = pl.BlockSpec(memory_space=pltpu.VMEM)
SMEM = pl.BlockSpec(memory_space=pltpu.SMEM)


def products(pieces, offsets, side, left, right, half):
    width = pieces[0].shape[1]
    height = half // 2
    count = len(pieces)
    scalars = jnp.stack(offsets + [side]).astype(jnp.int32)
    return pl.pallas_call(
        functools.partial(step_kernel, count),
        out_shape=(
            jax.ShapeDtypeStruct((height, width), F32),
            jax.ShapeDtypeStruct((height, width), BF16),
            jax.ShapeDtypeStruct((8, 128), F32),
        ),
        in_specs=[SMEM] + [VMEM] * (count + 2),
        out_specs=(VMEM, VMEM, VMEM),
        scratch_shapes=[
            pltpu.VMEM((width, width), BF16),
            pltpu.VMEM((half, right.shape[0]), BF16),
            pltpu.VMEM((half, width), F32),
        ],
        compiler_params=pltpu.CompilerParams(vmem_limit_bytes=STEP_VMEM),
    )(scalars, *pieces, left, right)


def small_inverse(entries, size):
    a = dict(entries)

    def get(i, j):
        return a[(i, j)] if i >= j else a[(j, i)]

    for p in range(0, size, 2):
        q = p + 1
        x, y, z = get(p, p), get(q, p), get(q, q)
        d = 1.0 / (x * z - y * y)
        xx, xy, yy = z * d, -(y * d), x * d
        rest = [i for i in range(size) if i not in (p, q)]
        old = {i: (get(i, p), get(i, q)) for i in rest}
        new = {i: (old[i][0] * xx + old[i][1] * xy, old[i][0] * xy + old[i][1] * yy) for i in rest}
        for n, i in enumerate(rest):
            for j in rest[: n + 1]:
                a[(i, j)] = a[(i, j)] - (new[i][0] * old[j][0] + new[i][1] * old[j][1])
        for i in rest:
            for k, j in ((0, p), (1, q)):
                a[(max(i, j), min(i, j))] = new[i][k]
        a[(p, p)], a[(q, p)], a[(q, q)] = -xx, -xy, -yy
    return {k: -v for k, v in a.items()}


def eliminate(m_ref, x_ref, y_ref, s_ref):
    size = m_ref.shape[0]
    lanes = lax.broadcasted_iota(jnp.int32, (8, size), 1)
    subs = lax.broadcasted_iota(jnp.int32, (8, size), 0)
    for b in range(size // 8):
        at = 8 * b
        base = (b % 2) * 64
        rows = m_ref[at : at + 8, :]
        for j in range(8):
            s_ref[base + 8 * j : base + 8 * j + 8, :] = jnp.broadcast_to(rows[:, at + j : at + j + 1], (8, 128))
        entries = {}
        for j in range(8):
            for i in range(j, 8):
                spot = base + 8 * j + i
                entries[(i, j)] = jnp.broadcast_to(s_ref[spot : spot + 1, :], (8, 128))
        inverse = small_inverse(entries, 8)
        inside = (lanes >= at) & (lanes < at + 8)
        rows = jnp.where(inside, (lanes - at == subs).astype(F32), rows)
        m_ref[at : at + 8, :] = rows
        single = [jnp.broadcast_to(m_ref[at + k : at + k + 1, :], (8, size)) for k in range(8)]
        solved = []
        for k in range(8):
            parts = []
            for h in range(0, size, 128):
                parts.append(tree([inverse[(max(k, n), min(k, n))] * single[n][:, h : h + 128] for n in range(8)]))
            solved.append(jnp.concatenate(parts, 1))
        merged = solved[0]
        for k in range(1, 8):
            merged = jnp.where(subs == k, solved[k], merged)
        done = lanes < at + 8
        x_ref[at : at + 8, :] = jnp.where(done, rows, 0.0)
        y_ref[at : at + 8, :] = jnp.where(done, merged, 0.0)
        for g in range(at + 8, size, 8):
            below = m_ref[g : g + 8, :]
            terms = [jnp.broadcast_to(below[:, at + k : at + k + 1], (8, size)) * solved[k] for k in range(8)]
            m_ref[g : g + 8, :] = jnp.where(inside, 0.0, below) - tree(terms)


def truncate_kernel(count, last, scalars, *refs):
    pieces = refs[:count]
    omega = refs[count]
    outs = refs[count + 1 : -9]
    y_ref, s_ref, high, low, cross, m_ref, x_ref, v_ref, spread = refs[-9:]
    width = y_ref.shape[1]
    size = m_ref.shape[0]
    scale = place(scalars, pieces, y_ref)
    at, rank = scalars[count], scalars[count + 1]
    sketch = matmul(y_ref[...], omega[...]) * scale
    s_ref[...] = sketch
    tall_high = sketch.astype(BF16)
    tall_low = (sketch - tall_high.astype(F32)).astype(BF16)
    turned = sketch.T
    high[...] = turned.astype(BF16)
    low[...] = (turned - high[...].astype(F32)).astype(BF16)
    gram = matmul(high[...], tall_high) + matmul(high[...], tall_low) + matmul(low[...], tall_high)
    row = lax.broadcasted_iota(jnp.int32, (size, size), 0)
    col = lax.broadcasted_iota(jnp.int32, (size, size), 1)
    m_ref[...] = jnp.where((row < rank) & (col < rank), gram, (row == col).astype(F32))
    cross[...] = (matmul(high[...], y_ref[...]) + matmul(low[...], y_ref[...])) * scale
    eliminate(m_ref, x_ref, v_ref, spread)
    kept = lax.broadcasted_iota(jnp.int32, (size, width), 0) < rank
    coeffs = jnp.where(kept, exact(v_ref[...], cross[...], ((1,), (0,))), 0.0)
    if last:
        result = outs[0]
        rows = result.shape[0]
        basis = exact(s_ref[pl.ds(pl.multiple_of(at, rows), rows), :], x_ref[...], ((1,), (1,)))
        result[...] = close(basis, coeffs).astype(BF16)
    else:
        middle, coeffs_out, basis_out = outs
        rows = middle.shape[0]
        coeffs_out[...] = coeffs.astype(BF16)
        basis_out[...] = exact(s_ref[...], x_ref[...], ((1,), (1,))).astype(BF16)
        middle[...] = matmul(basis_out[pl.ds(pl.multiple_of(at, rows), rows), :], coeffs_out[...]).astype(BF16)


def core_kernel(scalars, left, basis, small_a, small_b, spare):
    size = basis.shape[1]
    half = spare.shape[0] // (small_a.shape[0] // size)
    terms = small_a.shape[0] // size
    own = basis[pl.ds(pl.multiple_of(scalars[0], half), half), :]
    turned = own.astype(F32).T.astype(BF16)
    for i, small in ((1, small_b), (0, small_a)):
        part = terms * half
        spare[...] = matmul(left[i * part : (i + 1) * part, :], basis[...]).astype(BF16)
        for k in range(terms):
            value = matmul(turned, spare[k * half : (k + 1) * half, :])
            small[k * size : (k + 1) * size, :] = value.astype(small.dtype)


def core_matrices(left, start, half, basis):
    terms = left.shape[0] // half // 2
    size = basis.shape[1]
    return pl.pallas_call(
        core_kernel,
        out_shape=[
            jax.ShapeDtypeStruct((terms * size, size), F32),
            jax.ShapeDtypeStruct((terms * size, size), BF16),
        ],
        in_specs=[SMEM, VMEM, VMEM],
        out_specs=[VMEM] * 2,
        scratch_shapes=[pltpu.VMEM((terms * half, size), BF16)],
        compiler_params=pltpu.CompilerParams(vmem_limit_bytes=SMALL_VMEM),
    )(jnp.stack([start]).astype(jnp.int32), left, basis)


def next_kernel(scalars, left, small_a, small_b, part_a, part_b, out, coeffs, tall):
    size, width = coeffs.shape
    half = left.shape[0] // (2 * small_a.shape[0] // size)
    terms = small_a.shape[0] // size
    for at, part in ((scalars[0], part_a), (scalars[1], part_b)):
        coeffs[pl.ds(pl.multiple_of(at, size // 2), size // 2), :] = part[...]
    tall[...] = coeffs[...].astype(F32).T.astype(BF16)
    rows = tall[pl.ds(pl.multiple_of(scalars[2], half), half), :]
    for i, small in enumerate((small_a, small_b)):
        for k in range(terms):
            at = slice((i * terms + k) * half, (i * terms + k + 1) * half)
            spread = matmul(rows, small[k * size : (k + 1) * size, :]).astype(BF16)
            message = (matmul(spread, coeffs[...]) * (1.0 / width)).astype(BF16)
            out[at, :] = (left[at, :].astype(F32) + message.astype(F32)).astype(BF16)


def next_left(left, spots, smalls, parts):
    width = left.shape[1]
    size = 2 * parts[0].shape[0]
    return pl.pallas_call(
        next_kernel,
        out_shape=jax.ShapeDtypeStruct(left.shape, BF16),
        in_specs=[SMEM] + [VMEM] * 5,
        out_specs=VMEM,
        scratch_shapes=[pltpu.VMEM((size, width), BF16), pltpu.VMEM((width, size), BF16)],
        compiler_params=pltpu.CompilerParams(vmem_limit_bytes=SMALL_VMEM),
    )(jnp.stack(spots).astype(jnp.int32), left, *smalls, *parts)


def truncate(pieces, offsets, at, rank, omega, rows, last):
    width = pieces[0].shape[1]
    size = omega.shape[1]
    count = len(pieces)
    scalars = jnp.stack(offsets + [at, rank]).astype(jnp.int32)
    shapes = [jax.ShapeDtypeStruct((rows, width), BF16)]
    if not last:
        shapes += [jax.ShapeDtypeStruct((size, width), BF16), jax.ShapeDtypeStruct((width, size), BF16)]
    return pl.pallas_call(
        functools.partial(truncate_kernel, count, last),
        out_shape=tuple(shapes),
        in_specs=[SMEM] + [VMEM] * (count + 1),
        out_specs=tuple([VMEM] * len(shapes)),
        scratch_shapes=[
            pltpu.VMEM((width, width), BF16),
            pltpu.VMEM((width, size), F32),
            pltpu.VMEM((size, width), BF16),
            pltpu.VMEM((size, width), BF16),
            pltpu.VMEM((size, width), F32),
            pltpu.VMEM((size, size), F32),
            pltpu.VMEM((size, size), F32),
            pltpu.VMEM((size, size), F32),
            pltpu.VMEM((128, 128), F32),
        ],
        compiler_params=pltpu.CompilerParams(vmem_limit_bytes=CUT_VMEM),
    )(scalars, *pieces, omega)


def half_sweep(places, own, left, right, half, side):
    pieces, offsets = places.gather(own)
    previous = None
    for step in range(2):
        mine, other, scale = products(pieces, offsets, side, left, right, half)
        total = mine + places.side(other).astype(F32)
        shifted = own.astype(F32) - TAU * total
        if previous is not None:
            shifted = scale[:1, :1] * shifted - MOMENTUM * previous.astype(F32)
        own, previous = shifted.astype(BF16), own
        pieces, offsets = places.gather(own)
    return pieces, offsets


def on_device(places, state, left_env, right_env, inv_singular, sketch_cols, kept_ranks):
    rows = state[0]
    left = left_env[0]
    right = right_env[0]
    scales = inv_singular[0][None, :]
    rank = kept_ranks[0]
    width = rows.shape[1]
    terms = left.shape[0]
    m = lax.axis_index("mpo")
    side, core = m // 2, m % 2
    c = lax.axis_index("sec")
    half = rows.shape[0] // 2
    height = half // 2
    at = core * half + side * height

    own = lax.dynamic_slice(rows, (at, 0), (height, width))
    behind = places.shift(own, 1)
    merged = (own.astype(F32) + behind.astype(F32) * scales).astype(BF16)
    pair = places.core(left)
    left = jnp.concatenate([lax.dynamic_slice(a, (0, core * half, 0), (terms, half, width)) for a in (left, pair)])
    left = left.reshape(-1, width)
    right = jnp.concatenate([right, places.core(right)]).reshape(-1, width)
    start = c * (2 * half) + core * half
    pieces, offsets = half_sweep(places, merged, left, right, half, side)
    middle, coeffs, basis = truncate(
        pieces, offsets, start + side * height, rank, sketch_cols[0, 0], height, False
    )
    size = coeffs.shape[0]
    small_a, small_b = core_matrices(left, start, half, basis)
    small = small_a + places.core(small_b).astype(F32)
    ahead = places.shift(middle, -1)
    part = places.shift(lax.dynamic_slice(coeffs, (core * (size // 2), 0), (size // 2, width)), 1)
    small = places.sec_sum(small.astype(BF16))
    small, ahead, part = lax.optimization_barrier((small, ahead, part))
    small_in = places.shift(small, 1)
    merged = (middle.astype(F32) + ahead.astype(F32) * scales).astype(BF16)
    spots = [core * (size // 2), (1 - core) * (size // 2), start]
    left = next_left(left, spots, [small_in, places.core(small_in)], [part, places.core(part)])
    pieces, offsets = half_sweep(places, merged, left, right, half, side)
    (final_rows,) = truncate(pieces, offsets, c * (2 * half), rank, sketch_cols[0, 1], 2 * half, True)
    return final_rows[None]


def solution(mesh):
    places = Places(mesh)

    def run(*arrays):
        return on_device(places, *arrays)

    return jax.shard_map(
        run,
        mesh=mesh,
        in_specs=(
            P("seg", "sec", None),
            P("seg", "mpo", "sec", None),
            P("seg", "mpo", None, None),
            P("seg", None),
            P("seg", None, None, None),
            P("seg"),
        ),
        out_specs=P("seg", "sec", None),
        check_vma=False,
    )
```

```python
import functools

import jax
import jax.numpy as jnp
from jax import lax
from jax.experimental import pallas as pl
from jax.experimental.pallas import tpu as pltpu
from jax.sharding import PartitionSpec as P

TAU = 0.3
MOMENTUM = 0.5
EPS = 1e-06
F32 = jnp.float32
BF16 = jnp.bfloat16
AXES = ("seg", "mpo", "sec")


class Places:
    def __init__(self, mesh):
        self.segs = mesh.shape["seg"]
        self.mpo = mesh.shape["mpo"]
        self.secs = mesh.shape["sec"]

    def route(self, block, target):
        pairs = []
        for s in range(self.segs):
            for m in range(self.mpo):
                for c in range(self.secs):
                    t, n, d = target(s, m, c)
                    if 0 <= t < self.segs:
                        here = (s * self.mpo + m) * self.secs + c
                        pairs.append((here, (t * self.mpo + n) * self.secs + d))
        return lax.ppermute(block, AXES, pairs)

    def core(self, block):
        return self.route(block, lambda s, m, c: (s, m ^ 1, c))

    def side(self, block):
        return self.route(block, lambda s, m, c: (s, m ^ 2, c))

    def shift(self, block, distance):
        return self.route(block, lambda s, m, c: (s + distance, m, c))

    def sec(self, block):
        return self.route(block, lambda s, m, c: (s, m, c ^ 1))

    def diagonal(self, block):
        return self.route(block, lambda s, m, c: (s, m ^ 2, c ^ 1))

    def sec_sum(self, block):
        if self.secs == 2:
            return block + self.sec(block)
        return lax.psum(block, "sec")

    def gather(self, block):
        m = lax.axis_index("mpo")
        side, core = m // 2, m % 2
        c = lax.axis_index("sec")
        height, width = block.shape
        if self.secs == 2:
            sent = [(0, 0, block), (0, 1, self.side(block)), (1, 0, self.sec(block)), (1, 1, self.diagonal(block))]
            pieces, offsets = [], []
            for dc, dx, piece in sent:
                for dk, part in ((0, piece), (1, self.core(piece))):
                    pieces.append(part)
                    offsets.append((((c ^ dc) * 2 + (core ^ dk)) * 2 + (side ^ dx)) * height)
            return pieces, offsets
        column = lax.all_gather(block, "sec", axis=0, tiled=False)
        whole = jnp.zeros((self.secs, 2, 2, height, width), block.dtype)
        for dx, piece in ((0, column), (1, self.side(column))):
            for dk, part in ((0, piece), (1, self.core(piece))):
                whole = lax.dynamic_update_slice(whole, part[:, None, None], (0, core ^ dk, side ^ dx, 0, 0))
        return [whole.reshape(-1, width)], [jnp.int32(0)]


def matmul(a, b):
    return jnp.dot(a, b, preferred_element_type=F32)


def exact(a, b, contract):
    return lax.dot_general(a, b, (contract, ((), ())), precision=lax.Precision.HIGHEST, preferred_element_type=F32)


def split(a):
    high = a.astype(BF16)
    return high, (a - high.astype(F32)).astype(BF16)


def close(a, b):
    a_high, a_low = split(a)
    b_high, b_low = split(b)
    return matmul(a_high, b_high) + matmul(a_high, b_low) + matmul(a_low, b_high)


def tree(terms):
    while len(terms) > 1:
        paired = [terms[i] + terms[i + 1] for i in range(0, len(terms) - 1, 2)]
        terms = paired + terms[len(paired) * 2 :]
    return terms[0]


def place(offsets, pieces, y_ref):
    squares = None
    for i, piece in enumerate(pieces):
        height = piece.shape[0]
        at = pl.multiple_of(offsets[i], height) if height < y_ref.shape[0] else 0
        y_ref[pl.ds(at, height), :] = piece[...]
    for r in range(0, y_ref.shape[0], 128):
        big = y_ref[r : r + 128, :].astype(F32)
        part = jnp.sum(big * big, axis=0, keepdims=True)
        squares = part if squares is None else squares + part
    return y_ref.shape[1] * lax.rsqrt(jnp.sum(squares, axis=1, keepdims=True) + EPS)


def step_kernel(count, offsets, *refs):
    pieces = refs[:count]
    left, right, mine, other, scale, y_ref, first, sums = refs[count:]
    width = y_ref.shape[1]
    half = sums.shape[0]
    height = mine.shape[0]
    terms = left.shape[0] // half
    scale[...] = jnp.broadcast_to(place(offsets, pieces, y_ref), scale.shape)
    chunk = width // 2

    def forward(n, carry):
        cols = pl.ds(pl.multiple_of(n * chunk, chunk), chunk)
        for i in range(2):
            part = terms // 2 * half
            value = matmul(left[i * part : (i + 1) * part, :], y_ref[:, cols]).astype(BF16)
            for k in range(terms // 2):
                to = pl.multiple_of((i * (terms // 2) + k) * width + n * chunk, chunk)
                first[:, pl.ds(to, chunk)] = value[k * half : (k + 1) * half]
        return carry

    lax.fori_loop(0, 2, forward, 0)

    def back(n, carry):
        cols = pl.ds(pl.multiple_of(n * chunk, chunk), chunk)
        sums[:, cols] = matmul(first[...], right[:, cols])
        return carry

    lax.fori_loop(0, 2, back, 0)
    side = offsets[count]
    mine[...] = sums[pl.ds(pl.multiple_of(side * height, height), height), :]
    other[...] = sums[pl.ds(pl.multiple_of((1 - side) * height, height), height), :].astype(BF16)


STEP_VMEM = 20 << 20
SMALL_VMEM = 12 << 20
CUT_VMEM = 14 << 20
VMEM = pl.BlockSpec(memory_space=pltpu.VMEM)
SMEM = pl.BlockSpec(memory_space=pltpu.SMEM)


def products(pieces, offsets, side, left, right, half):
    width = pieces[0].shape[1]
    height = half // 2
    count = len(pieces)
    scalars = jnp.stack(offsets + [side]).astype(jnp.int32)
    return pl.pallas_call(
        functools.partial(step_kernel, count),
        out_shape=(
            jax.ShapeDtypeStruct((height, width), F32),
            jax.ShapeDtypeStruct((height, width), BF16),
            jax.ShapeDtypeStruct((8, 128), F32),
        ),
        in_specs=[SMEM] + [VMEM] * (count + 2),
        out_specs=(VMEM, VMEM, VMEM),
        scratch_shapes=[
            pltpu.VMEM((width, width), BF16),
            pltpu.VMEM((half, right.shape[0]), BF16),
            pltpu.VMEM((half, width), F32),
        ],
        compiler_params=pltpu.CompilerParams(vmem_limit_bytes=STEP_VMEM),
    )(scalars, *pieces, left, right)


def small_inverse(entries, size):
    a = dict(entries)

    def get(i, j):
        return a[(i, j)] if i >= j else a[(j, i)]

    for p in range(0, size, 2):
        q = p + 1
        x, y, z = get(p, p), get(q, p), get(q, q)
        d = 1.0 / (x * z - y * y)
        xx, xy, yy = z * d, -(y * d), x * d
        rest = [i for i in range(size) if i not in (p, q)]
        old = {i: (get(i, p), get(i, q)) for i in rest}
        new = {i: (old[i][0] * xx + old[i][1] * xy, old[i][0] * xy + old[i][1] * yy) for i in rest}
        for n, i in enumerate(rest):
            for j in rest[: n + 1]:
                a[(i, j)] = a[(i, j)] - (new[i][0] * old[j][0] + new[i][1] * old[j][1])
        for i in rest:
            for k, j in ((0, p), (1, q)):
                a[(max(i, j), min(i, j))] = new[i][k]
        a[(p, p)], a[(q, p)], a[(q, q)] = -xx, -xy, -yy
    return {k: -v for k, v in a.items()}


def eliminate(m_ref, x_ref, y_ref, s_ref):
    size = m_ref.shape[0]
    lanes = lax.broadcasted_iota(jnp.int32, (8, size), 1)
    subs = lax.broadcasted_iota(jnp.int32, (8, size), 0)
    for b in range(size // 8):
        at = 8 * b
        base = (b % 2) * 64
        rows = m_ref[at : at + 8, :]
        for j in range(8):
            s_ref[base + 8 * j : base + 8 * j + 8, :] = jnp.broadcast_to(rows[:, at + j : at + j + 1], (8, 128))
        entries = {}
        for j in range(8):
            for i in range(j, 8):
                spot = base + 8 * j + i
                entries[(i, j)] = jnp.broadcast_to(s_ref[spot : spot + 1, :], (8, 128))
        inverse = small_inverse(entries, 8)
        inside = (lanes >= at) & (lanes < at + 8)
        rows = jnp.where(inside, (lanes - at == subs).astype(F32), rows)
        m_ref[at : at + 8, :] = rows
        single = [jnp.broadcast_to(m_ref[at + k : at + k + 1, :], (8, size)) for k in range(8)]
        solved = []
        for k in range(8):
            parts = []
            for h in range(0, size, 128):
                parts.append(tree([inverse[(max(k, n), min(k, n))] * single[n][:, h : h + 128] for n in range(8)]))
            solved.append(jnp.concatenate(parts, 1) if len(parts) > 1 else parts[0])
        merged = solved[0]
        for k in range(1, 8):
            merged = jnp.where(subs == k, solved[k], merged)
        done = lanes < at + 8
        x_ref[at : at + 8, :] = jnp.where(done, rows, 0.0)
        y_ref[at : at + 8, :] = jnp.where(done, merged, 0.0)
        for g in range(at + 8, size, 8):
            below = m_ref[g : g + 8, :]
            terms = [jnp.broadcast_to(below[:, at + k : at + k + 1], (8, size)) * solved[k] for k in range(8)]
            m_ref[g : g + 8, :] = jnp.where(inside, 0.0, below) - tree(terms)


def eliminate_halves(m_ref, x_ref, y_ref, s_ref, part, x_part, y_part, kept):
    half = part.shape[0]
    upper, lower = slice(0, half), slice(half, 2 * half)
    plain, turned = ((1,), (0,)), ((0,), (0,))
    part[...] = m_ref[upper, upper]
    eliminate(part, x_part, y_part, s_ref)
    left = exact(x_part[...], m_ref[upper, lower], plain)
    right = exact(y_part[...], m_ref[upper, lower], plain)
    kept[...] = exact(left, y_part[...], turned)
    part[...] = m_ref[lower, lower] - exact(left, right, turned)
    for full, own in ((x_ref, x_part), (y_ref, y_part)):
        full[upper, upper] = own[...]
        full[upper, lower] = jnp.zeros((half, half), F32)
    eliminate(part, x_part, y_part, s_ref)
    for full, own in ((x_ref, x_part), (y_ref, y_part)):
        full[lower, lower] = own[...]
        full[lower, upper] = -exact(own[...], kept[...], plain)


def truncate_kernel(count, last, scalars, *refs):
    pieces = refs[:count]
    omega = refs[count]
    outs = refs[count + 1 : -13]
    y_ref, s_ref, high, low, cross, m_ref, x_ref, v_ref, spread = refs[-13:-4]
    width = y_ref.shape[1]
    size = m_ref.shape[0]
    scale = place(scalars, pieces, y_ref)
    at, rank = scalars[count], scalars[count + 1]
    sketch = matmul(y_ref[...], omega[...]) * scale
    s_ref[...] = sketch
    tall_high = sketch.astype(BF16)
    tall_low = (sketch - tall_high.astype(F32)).astype(BF16)
    turned = sketch.T
    high[...] = turned.astype(BF16)
    low[...] = (turned - high[...].astype(F32)).astype(BF16)
    gram = matmul(high[...], tall_high) + matmul(high[...], tall_low) + matmul(low[...], tall_high)
    row = lax.broadcasted_iota(jnp.int32, (size, size), 0)
    col = lax.broadcasted_iota(jnp.int32, (size, size), 1)
    m_ref[...] = jnp.where((row < rank) & (col < rank), gram, (row == col).astype(F32))
    cross[...] = (matmul(high[...], y_ref[...]) + matmul(low[...], y_ref[...])) * scale
    eliminate_halves(m_ref, x_ref, v_ref, spread, *refs[-4:])
    kept = lax.broadcasted_iota(jnp.int32, (size, width), 0) < rank
    coeffs = jnp.where(kept, exact(v_ref[...], cross[...], ((1,), (0,))), 0.0)
    if last:
        result = outs[0]
        rows = result.shape[0]
        basis = exact(s_ref[pl.ds(pl.multiple_of(at, rows), rows), :], x_ref[...], ((1,), (1,)))
        result[...] = close(basis, coeffs).astype(BF16)
    else:
        middle, coeffs_out, basis_out = outs
        rows = middle.shape[0]
        coeffs_out[...] = coeffs.astype(BF16)
        basis_out[...] = exact(s_ref[...], x_ref[...], ((1,), (1,))).astype(BF16)
        middle[...] = matmul(basis_out[pl.ds(pl.multiple_of(at, rows), rows), :], coeffs_out[...]).astype(BF16)


def core_kernel(scalars, left, basis, small_a, small_b, spare):
    size = basis.shape[1]
    half = spare.shape[0] // (small_a.shape[0] // size)
    terms = small_a.shape[0] // size
    own = basis[pl.ds(pl.multiple_of(scalars[0], half), half), :]
    turned = own.astype(F32).T.astype(BF16)
    for i, small in ((1, small_b), (0, small_a)):
        part = terms * half
        spare[...] = matmul(left[i * part : (i + 1) * part, :], basis[...]).astype(BF16)
        for k in range(terms):
            value = matmul(turned, spare[k * half : (k + 1) * half, :])
            small[k * size : (k + 1) * size, :] = value.astype(small.dtype)


def core_matrices(left, start, half, basis):
    terms = left.shape[0] // half // 2
    size = basis.shape[1]
    return pl.pallas_call(
        core_kernel,
        out_shape=[
            jax.ShapeDtypeStruct((terms * size, size), F32),
            jax.ShapeDtypeStruct((terms * size, size), BF16),
        ],
        in_specs=[SMEM, VMEM, VMEM],
        out_specs=[VMEM] * 2,
        scratch_shapes=[pltpu.VMEM((terms * half, size), BF16)],
        compiler_params=pltpu.CompilerParams(vmem_limit_bytes=SMALL_VMEM),
    )(jnp.stack([start]).astype(jnp.int32), left, basis)


def next_kernel(scalars, left, small_a, small_b, part_a, part_b, out, coeffs, tall):
    size, width = coeffs.shape
    half = left.shape[0] // (2 * small_a.shape[0] // size)
    terms = small_a.shape[0] // size
    for at, part in ((scalars[0], part_a), (scalars[1], part_b)):
        coeffs[pl.ds(pl.multiple_of(at, size // 2), size // 2), :] = part[...]
    tall[...] = coeffs[...].astype(F32).T.astype(BF16)
    rows = tall[pl.ds(pl.multiple_of(scalars[2], half), half), :]
    for i, small in enumerate((small_a, small_b)):
        for k in range(terms):
            at = slice((i * terms + k) * half, (i * terms + k + 1) * half)
            spread = matmul(rows, small[k * size : (k + 1) * size, :]).astype(BF16)
            message = (matmul(spread, coeffs[...]) * (1.0 / width)).astype(BF16)
            out[at, :] = (left[at, :].astype(F32) + message.astype(F32)).astype(BF16)


def next_left(left, spots, smalls, parts):
    width = left.shape[1]
    size = 2 * parts[0].shape[0]
    return pl.pallas_call(
        next_kernel,
        out_shape=jax.ShapeDtypeStruct(left.shape, BF16),
        in_specs=[SMEM] + [VMEM] * 5,
        out_specs=VMEM,
        scratch_shapes=[pltpu.VMEM((size, width), BF16), pltpu.VMEM((width, size), BF16)],
        compiler_params=pltpu.CompilerParams(vmem_limit_bytes=SMALL_VMEM),
    )(jnp.stack(spots).astype(jnp.int32), left, *smalls, *parts)


def truncate(pieces, offsets, at, rank, omega, rows, last):
    width = pieces[0].shape[1]
    size = omega.shape[1]
    count = len(pieces)
    scalars = jnp.stack(offsets + [at, rank]).astype(jnp.int32)
    shapes = [jax.ShapeDtypeStruct((rows, width), BF16)]
    if not last:
        shapes += [jax.ShapeDtypeStruct((size, width), BF16), jax.ShapeDtypeStruct((width, size), BF16)]
    return pl.pallas_call(
        functools.partial(truncate_kernel, count, last),
        out_shape=tuple(shapes),
        in_specs=[SMEM] + [VMEM] * (count + 1),
        out_specs=tuple([VMEM] * len(shapes)),
        scratch_shapes=[
            pltpu.VMEM((width, width), BF16),
            pltpu.VMEM((width, size), F32),
            pltpu.VMEM((size, width), BF16),
            pltpu.VMEM((size, width), BF16),
            pltpu.VMEM((size, width), F32),
            pltpu.VMEM((size, size), F32),
            pltpu.VMEM((size, size), F32),
            pltpu.VMEM((size, size), F32),
            pltpu.VMEM((128, 128), F32),
        ]
        + [pltpu.VMEM((size // 2, size // 2), F32)] * 4,
        compiler_params=pltpu.CompilerParams(vmem_limit_bytes=CUT_VMEM),
    )(scalars, *pieces, omega)


def half_sweep(places, own, left, right, half, side):
    pieces, offsets = places.gather(own)
    previous = None
    for step in range(2):
        mine, other, scale = products(pieces, offsets, side, left, right, half)
        total = mine + places.side(other).astype(F32)
        shifted = own.astype(F32) - TAU * total
        if previous is not None:
            shifted = scale[:1, :1] * shifted - MOMENTUM * previous.astype(F32)
        own, previous = shifted.astype(BF16), own
        pieces, offsets = places.gather(own)
    return pieces, offsets


def on_device(places, state, left_env, right_env, inv_singular, sketch_cols, kept_ranks):
    rows = state[0]
    left = left_env[0]
    right = right_env[0]
    scales = inv_singular[0][None, :]
    rank = kept_ranks[0]
    width = rows.shape[1]
    terms = left.shape[0]
    m = lax.axis_index("mpo")
    side, core = m // 2, m % 2
    c = lax.axis_index("sec")
    half = rows.shape[0] // 2
    height = half // 2
    at = core * half + side * height

    own = lax.dynamic_slice(rows, (at, 0), (height, width))
    behind = places.shift(own, 1)
    merged = (own.astype(F32) + behind.astype(F32) * scales).astype(BF16)
    pair = places.core(left)
    left = jnp.concatenate([lax.dynamic_slice(a, (0, core * half, 0), (terms, half, width)) for a in (left, pair)])
    left = left.reshape(-1, width)
    right = jnp.concatenate([right, places.core(right)]).reshape(-1, width)
    start = c * (2 * half) + core * half
    pieces, offsets = half_sweep(places, merged, left, right, half, side)
    middle, coeffs, basis = truncate(
        pieces, offsets, start + side * height, rank, sketch_cols[0, 0], height, False
    )
    size = coeffs.shape[0]
    small_a, small_b = core_matrices(left, start, half, basis)
    small = small_a + places.core(small_b).astype(F32)
    ahead = places.shift(middle, -1)
    part = places.shift(lax.dynamic_slice(coeffs, (core * (size // 2), 0), (size // 2, width)), 1)
    small = places.sec_sum(small.astype(BF16))
    small, ahead, part = lax.optimization_barrier((small, ahead, part))
    small_in = places.shift(small, 1)
    merged = (middle.astype(F32) + ahead.astype(F32) * scales).astype(BF16)
    spots = [core * (size // 2), (1 - core) * (size // 2), start]
    left = next_left(left, spots, [small_in, places.core(small_in)], [part, places.core(part)])
    pieces, offsets = half_sweep(places, merged, left, right, half, side)
    (final_rows,) = truncate(pieces, offsets, c * (2 * half), rank, sketch_cols[0, 1], 2 * half, True)
    return final_rows[None]


def solution(mesh):
    places = Places(mesh)

    def run(*arrays):
        return on_device(places, *arrays)

    return jax.shard_map(
        run,
        mesh=mesh,
        in_specs=(
            P("seg", "sec", None),
            P("seg", "mpo", "sec", None),
            P("seg", "mpo", None, None),
            P("seg", None),
            P("seg", None, None, None),
            P("seg"),
        ),
        out_specs=P("seg", "sec", None),
        check_vma=False,
    )
```

```python
import functools

import jax
import jax.numpy as jnp
from jax import lax
from jax.experimental import pallas as pl
from jax.experimental.pallas import tpu as pltpu
from jax.sharding import PartitionSpec as P

TAU = 0.3
MOMENTUM = 0.5
EPS = 1e-06
F32 = jnp.float32
BF16 = jnp.bfloat16
AXES = ("seg", "mpo", "sec")


class Places:
    def __init__(self, mesh):
        self.segs = mesh.shape["seg"]
        self.mpo = mesh.shape["mpo"]
        self.secs = mesh.shape["sec"]

    def route(self, block, target):
        pairs = []
        for s in range(self.segs):
            for m in range(self.mpo):
                for c in range(self.secs):
                    t, n, d = target(s, m, c)
                    if 0 <= t < self.segs:
                        here = (s * self.mpo + m) * self.secs + c
                        pairs.append((here, (t * self.mpo + n) * self.secs + d))
        return lax.ppermute(block, AXES, pairs)

    def core(self, block):
        return self.route(block, lambda s, m, c: (s, m ^ 1, c))

    def side(self, block):
        return self.route(block, lambda s, m, c: (s, m ^ 2, c))

    def shift(self, block, distance):
        return self.route(block, lambda s, m, c: (s + distance, m, c))

    def sec(self, block):
        return self.route(block, lambda s, m, c: (s, m, c ^ 1))

    def diagonal(self, block):
        return self.route(block, lambda s, m, c: (s, m ^ 2, c ^ 1))

    def sec_sum(self, block):
        if self.secs == 2:
            return block + self.sec(block)
        return lax.psum(block, "sec")

    def gather(self, block):
        m = lax.axis_index("mpo")
        side, core = m // 2, m % 2
        c = lax.axis_index("sec")
        height, width = block.shape
        if self.secs == 2:
            sent = [(0, 0, block), (0, 1, self.side(block)), (1, 0, self.sec(block)), (1, 1, self.diagonal(block))]
            pieces, offsets = [], []
            for dc, dx, piece in sent:
                for dk, part in ((0, piece), (1, self.core(piece))):
                    pieces.append(part)
                    offsets.append((((c ^ dc) * 2 + (core ^ dk)) * 2 + (side ^ dx)) * height)
            return pieces, offsets
        column = lax.all_gather(block, "sec", axis=0, tiled=False)
        whole = jnp.zeros((self.secs, 2, 2, height, width), block.dtype)
        for dx, piece in ((0, column), (1, self.side(column))):
            for dk, part in ((0, piece), (1, self.core(piece))):
                whole = lax.dynamic_update_slice(whole, part[:, None, None], (0, core ^ dk, side ^ dx, 0, 0))
        return [whole.reshape(-1, width)], [jnp.int32(0)]


def matmul(a, b):
    return jnp.dot(a, b, preferred_element_type=F32)


def exact(a, b, contract):
    return lax.dot_general(a, b, (contract, ((), ())), precision=lax.Precision.HIGHEST, preferred_element_type=F32)


def split(a):
    high = a.astype(BF16)
    return high, (a - high.astype(F32)).astype(BF16)


def close(a, b):
    a_high, a_low = split(a)
    b_high, b_low = split(b)
    return matmul(a_high, b_high) + matmul(a_high, b_low) + matmul(a_low, b_high)


def tree(terms):
    while len(terms) > 1:
        paired = [terms[i] + terms[i + 1] for i in range(0, len(terms) - 1, 2)]
        terms = paired + terms[len(paired) * 2 :]
    return terms[0]


def place(offsets, pieces, y_ref):
    squares = None
    for i, piece in enumerate(pieces):
        height = piece.shape[0]
        at = pl.multiple_of(offsets[i], height) if height < y_ref.shape[0] else 0
        y_ref[pl.ds(at, height), :] = piece[...]
    for r in range(0, y_ref.shape[0], 128):
        big = y_ref[r : r + 128, :].astype(F32)
        part = jnp.sum(big * big, axis=0, keepdims=True)
        squares = part if squares is None else squares + part
    return y_ref.shape[1] * lax.rsqrt(jnp.sum(squares, axis=1, keepdims=True) + EPS)


def step_kernel(count, offsets, *refs):
    pieces = refs[:count]
    left, right, mine, other, scale, y_ref, first, sums = refs[count:]
    width = y_ref.shape[1]
    half = sums.shape[0]
    height = mine.shape[0]
    terms = left.shape[0] // half
    scale[...] = jnp.broadcast_to(place(offsets, pieces, y_ref), scale.shape)
    chunk = width // 2

    part = terms // 2 * half

    def forward(j, carry):
        n, i = j // 2, j % 2
        cols = pl.ds(pl.multiple_of(n * chunk, chunk), chunk)
        value = matmul(left[pl.ds(pl.multiple_of(i * part, part), part), :], y_ref[:, cols]).astype(BF16)
        for k in range(terms // 2):
            to = pl.multiple_of((i * (terms // 2) + k) * width + n * chunk, chunk)
            first[:, pl.ds(to, chunk)] = value[k * half : (k + 1) * half]
        return carry

    lax.fori_loop(0, 4, forward, 0)

    def back(n, carry):
        cols = pl.ds(pl.multiple_of(n * chunk, chunk), chunk)
        sums[:, cols] = matmul(first[...], right[:, cols])
        return carry

    lax.fori_loop(0, 2, back, 0)
    side = offsets[count]
    mine[...] = sums[pl.ds(pl.multiple_of(side * height, height), height), :]
    other[...] = sums[pl.ds(pl.multiple_of((1 - side) * height, height), height), :].astype(BF16)


STEP_VMEM = 20 << 20
SMALL_VMEM = 12 << 20
CUT_VMEM = 14 << 20
VMEM = pl.BlockSpec(memory_space=pltpu.VMEM)
SMEM = pl.BlockSpec(memory_space=pltpu.SMEM)


def products(pieces, offsets, side, left, right, half):
    width = pieces[0].shape[1]
    height = half // 2
    count = len(pieces)
    scalars = jnp.stack(offsets + [side]).astype(jnp.int32)
    return pl.pallas_call(
        functools.partial(step_kernel, count),
        out_shape=(
            jax.ShapeDtypeStruct((height, width), F32),
            jax.ShapeDtypeStruct((height, width), BF16),
            jax.ShapeDtypeStruct((8, 128), F32),
        ),
        in_specs=[SMEM] + [VMEM] * (count + 2),
        out_specs=(VMEM, VMEM, VMEM),
        scratch_shapes=[
            pltpu.VMEM((width, width), BF16),
            pltpu.VMEM((half, right.shape[0]), BF16),
            pltpu.VMEM((half, width), F32),
        ],
        compiler_params=pltpu.CompilerParams(vmem_limit_bytes=STEP_VMEM),
    )(scalars, *pieces, left, right)


def small_inverse(entries, size):
    a = dict(entries)

    def get(i, j):
        return a[(i, j)] if i >= j else a[(j, i)]

    for p in range(0, size, 2):
        q = p + 1
        x, y, z = get(p, p), get(q, p), get(q, q)
        d = 1.0 / (x * z - y * y)
        xx, xy, yy = z * d, -(y * d), x * d
        rest = [i for i in range(size) if i not in (p, q)]
        old = {i: (get(i, p), get(i, q)) for i in rest}
        new = {i: (old[i][0] * xx + old[i][1] * xy, old[i][0] * xy + old[i][1] * yy) for i in rest}
        for n, i in enumerate(rest):
            for j in rest[: n + 1]:
                a[(i, j)] = a[(i, j)] - (new[i][0] * old[j][0] + new[i][1] * old[j][1])
        for i in rest:
            for k, j in ((0, p), (1, q)):
                a[(max(i, j), min(i, j))] = new[i][k]
        a[(p, p)], a[(q, p)], a[(q, q)] = -xx, -xy, -yy
    return {k: -v for k, v in a.items()}


def eliminate(m_ref, x_ref, y_ref, s_ref):
    size = m_ref.shape[0]
    lanes = lax.broadcasted_iota(jnp.int32, (8, size), 1)
    subs = lax.broadcasted_iota(jnp.int32, (8, size), 0)
    for b in range(size // 8):
        at = 8 * b
        base = (b % 2) * 64
        rows = m_ref[at : at + 8, :]
        for j in range(8):
            s_ref[base + 8 * j : base + 8 * j + 8, :] = jnp.broadcast_to(rows[:, at + j : at + j + 1], (8, 128))
        entries = {}
        for j in range(8):
            for i in range(j, 8):
                spot = base + 8 * j + i
                entries[(i, j)] = jnp.broadcast_to(s_ref[spot : spot + 1, :], (8, 128))
        inverse = small_inverse(entries, 8)
        inside = (lanes >= at) & (lanes < at + 8)
        rows = jnp.where(inside, (lanes - at == subs).astype(F32), rows)
        m_ref[at : at + 8, :] = rows
        single = [jnp.broadcast_to(m_ref[at + k : at + k + 1, :], (8, size)) for k in range(8)]
        solved = []
        for k in range(8):
            parts = []
            for h in range(0, size, 128):
                parts.append(tree([inverse[(max(k, n), min(k, n))] * single[n][:, h : h + 128] for n in range(8)]))
            solved.append(jnp.concatenate(parts, 1) if len(parts) > 1 else parts[0])
        merged = solved[0]
        for k in range(1, 8):
            merged = jnp.where(subs == k, solved[k], merged)
        done = lanes < at + 8
        x_ref[at : at + 8, :] = jnp.where(done, rows, 0.0)
        y_ref[at : at + 8, :] = jnp.where(done, merged, 0.0)
        for g in range(at + 8, size, 8):
            below = m_ref[g : g + 8, :]
            terms = [jnp.broadcast_to(below[:, at + k : at + k + 1], (8, size)) * solved[k] for k in range(8)]
            m_ref[g : g + 8, :] = jnp.where(inside, 0.0, below) - tree(terms)


def eliminate_halves(m_ref, x_ref, y_ref, s_ref, part, x_part, y_part, kept):
    half = part.shape[0]
    upper, lower = slice(0, half), slice(half, 2 * half)
    plain, turned = ((1,), (0,)), ((0,), (0,))
    part[...] = m_ref[upper, upper]
    for full in (x_ref, y_ref):
        full[upper, lower] = jnp.zeros((half, half), F32)

    def stage(i, carry):
        eliminate(part, x_part, y_part, s_ref)

        @pl.when(i == 0)
        def _():
            left = exact(x_part[...], m_ref[upper, lower], plain)
            right = exact(y_part[...], m_ref[upper, lower], plain)
            kept[...] = exact(left, y_part[...], turned)
            part[...] = m_ref[lower, lower] - exact(left, right, turned)
            for full, own in ((x_ref, x_part), (y_ref, y_part)):
                full[upper, upper] = own[...]

        @pl.when(i == 1)
        def _():
            for full, own in ((x_ref, x_part), (y_ref, y_part)):
                full[lower, lower] = own[...]
                full[lower, upper] = -exact(own[...], kept[...], plain)

        return carry

    lax.fori_loop(0, 2, stage, 0)


def truncate_kernel(count, last, scalars, *refs):
    pieces = refs[:count]
    omega = refs[count]
    outs = refs[count + 1 : -13]
    y_ref, s_ref, high, low, cross, m_ref, x_ref, v_ref, spread = refs[-13:-4]
    width = y_ref.shape[1]
    size = m_ref.shape[0]
    scale = place(scalars, pieces, y_ref)
    at, rank = scalars[count], scalars[count + 1]
    sketch = matmul(y_ref[...], omega[...]) * scale
    s_ref[...] = sketch
    tall_high = sketch.astype(BF16)
    tall_low = (sketch - tall_high.astype(F32)).astype(BF16)
    turned = sketch.T
    high[...] = turned.astype(BF16)
    low[...] = (turned - high[...].astype(F32)).astype(BF16)
    gram = matmul(high[...], tall_high) + matmul(high[...], tall_low) + matmul(low[...], tall_high)
    row = lax.broadcasted_iota(jnp.int32, (size, size), 0)
    col = lax.broadcasted_iota(jnp.int32, (size, size), 1)
    m_ref[...] = jnp.where((row < rank) & (col < rank), gram, (row == col).astype(F32))
    cross[...] = (matmul(high[...], y_ref[...]) + matmul(low[...], y_ref[...])) * scale
    eliminate_halves(m_ref, x_ref, v_ref, spread, *refs[-4:])
    kept = lax.broadcasted_iota(jnp.int32, (size, width), 0) < rank
    coeffs = jnp.where(kept, exact(v_ref[...], cross[...], ((1,), (0,))), 0.0)
    if last:
        result = outs[0]
        rows = result.shape[0]
        basis = exact(s_ref[pl.ds(pl.multiple_of(at, rows), rows), :], x_ref[...], ((1,), (1,)))
        result[...] = close(basis, coeffs).astype(BF16)
    else:
        middle, coeffs_out, basis_out = outs
        rows = middle.shape[0]
        coeffs_out[...] = coeffs.astype(BF16)
        basis_out[...] = exact(s_ref[...], x_ref[...], ((1,), (1,))).astype(BF16)
        middle[...] = matmul(basis_out[pl.ds(pl.multiple_of(at, rows), rows), :], coeffs_out[...]).astype(BF16)


def core_kernel(scalars, left, basis, small_a, small_b, spare):
    size = basis.shape[1]
    half = spare.shape[0] // (small_a.shape[0] // size)
    terms = small_a.shape[0] // size
    own = basis[pl.ds(pl.multiple_of(scalars[0], half), half), :]
    turned = own.astype(F32).T.astype(BF16)
    for i, small in ((1, small_b), (0, small_a)):
        part = terms * half
        spare[...] = matmul(left[i * part : (i + 1) * part, :], basis[...]).astype(BF16)
        for k in range(terms):
            value = matmul(turned, spare[k * half : (k + 1) * half, :])
            small[k * size : (k + 1) * size, :] = value.astype(small.dtype)


def core_matrices(left, start, half, basis):
    terms = left.shape[0] // half // 2
    size = basis.shape[1]
    return pl.pallas_call(
        core_kernel,
        out_shape=[
            jax.ShapeDtypeStruct((terms * size, size), F32),
            jax.ShapeDtypeStruct((terms * size, size), BF16),
        ],
        in_specs=[SMEM, VMEM, VMEM],
        out_specs=[VMEM] * 2,
        scratch_shapes=[pltpu.VMEM((terms * half, size), BF16)],
        compiler_params=pltpu.CompilerParams(vmem_limit_bytes=SMALL_VMEM),
    )(jnp.stack([start]).astype(jnp.int32), left, basis)


def next_kernel(scalars, left, small_a, small_b, part_a, part_b, out, coeffs, tall):
    size, width = coeffs.shape
    half = left.shape[0] // (2 * small_a.shape[0] // size)
    terms = small_a.shape[0] // size
    for at, part in ((scalars[0], part_a), (scalars[1], part_b)):
        coeffs[pl.ds(pl.multiple_of(at, size // 2), size // 2), :] = part[...]
    tall[...] = coeffs[...].astype(F32).T.astype(BF16)
    rows = tall[pl.ds(pl.multiple_of(scalars[2], half), half), :]
    for i, small in enumerate((small_a, small_b)):
        for k in range(terms):
            at = slice((i * terms + k) * half, (i * terms + k + 1) * half)
            spread = matmul(rows, small[k * size : (k + 1) * size, :]).astype(BF16)
            message = (matmul(spread, coeffs[...]) * (1.0 / width)).astype(BF16)
            out[at, :] = (left[at, :].astype(F32) + message.astype(F32)).astype(BF16)


def next_left(left, spots, smalls, parts):
    width = left.shape[1]
    size = 2 * parts[0].shape[0]
    return pl.pallas_call(
        next_kernel,
        out_shape=jax.ShapeDtypeStruct(left.shape, BF16),
        in_specs=[SMEM] + [VMEM] * 5,
        out_specs=VMEM,
        scratch_shapes=[pltpu.VMEM((size, width), BF16), pltpu.VMEM((width, size), BF16)],
        compiler_params=pltpu.CompilerParams(vmem_limit_bytes=SMALL_VMEM),
    )(jnp.stack(spots).astype(jnp.int32), left, *smalls, *parts)


def truncate(pieces, offsets, at, rank, omega, rows, last):
    width = pieces[0].shape[1]
    size = omega.shape[1]
    count = len(pieces)
    scalars = jnp.stack(offsets + [at, rank]).astype(jnp.int32)
    shapes = [jax.ShapeDtypeStruct((rows, width), BF16)]
    if not last:
        shapes += [jax.ShapeDtypeStruct((size, width), BF16), jax.ShapeDtypeStruct((width, size), BF16)]
    return pl.pallas_call(
        functools.partial(truncate_kernel, count, last),
        out_shape=tuple(shapes),
        in_specs=[SMEM] + [VMEM] * (count + 1),
        out_specs=tuple([VMEM] * len(shapes)),
        scratch_shapes=[
            pltpu.VMEM((width, width), BF16),
            pltpu.VMEM((width, size), F32),
            pltpu.VMEM((size, width), BF16),
            pltpu.VMEM((size, width), BF16),
            pltpu.VMEM((size, width), F32),
            pltpu.VMEM((size, size), F32),
            pltpu.VMEM((size, size), F32),
            pltpu.VMEM((size, size), F32),
            pltpu.VMEM((128, 128), F32),
        ]
        + [pltpu.VMEM((size // 2, size // 2), F32)] * 4,
        compiler_params=pltpu.CompilerParams(vmem_limit_bytes=CUT_VMEM),
    )(scalars, *pieces, omega)


def half_sweep(places, own, left, right, half, side):
    pieces, offsets = places.gather(own)
    previous = None
    for step in range(2):
        mine, other, scale = products(pieces, offsets, side, left, right, half)
        total = mine + places.side(other).astype(F32)
        shifted = own.astype(F32) - TAU * total
        if previous is not None:
            shifted = scale[:1, :1] * shifted - MOMENTUM * previous.astype(F32)
        own, previous = shifted.astype(BF16), own
        pieces, offsets = places.gather(own)
    return pieces, offsets


def on_device(places, state, left_env, right_env, inv_singular, sketch_cols, kept_ranks):
    rows = state[0]
    left = left_env[0]
    right = right_env[0]
    scales = inv_singular[0][None, :]
    rank = kept_ranks[0]
    width = rows.shape[1]
    terms = left.shape[0]
    m = lax.axis_index("mpo")
    side, core = m // 2, m % 2
    c = lax.axis_index("sec")
    half = rows.shape[0] // 2
    height = half // 2
    at = core * half + side * height

    own = lax.dynamic_slice(rows, (at, 0), (height, width))
    behind = places.shift(own, 1)
    merged = (own.astype(F32) + behind.astype(F32) * scales).astype(BF16)
    pair = places.core(left)
    left = jnp.concatenate([lax.dynamic_slice(a, (0, core * half, 0), (terms, half, width)) for a in (left, pair)])
    left = left.reshape(-1, width)
    right = jnp.concatenate([right, places.core(right)]).reshape(-1, width)
    start = c * (2 * half) + core * half
    pieces, offsets = half_sweep(places, merged, left, right, half, side)
    middle, coeffs, basis = truncate(
        pieces, offsets, start + side * height, rank, sketch_cols[0, 0], height, False
    )
    size = coeffs.shape[0]
    small_a, small_b = core_matrices(left, start, half, basis)
    small = small_a + places.core(small_b).astype(F32)
    ahead = places.shift(middle, -1)
    part = places.shift(lax.dynamic_slice(coeffs, (core * (size // 2), 0), (size // 2, width)), 1)
    small = places.sec_sum(small.astype(BF16))
    small, ahead, part = lax.optimization_barrier((small, ahead, part))
    small_in = places.shift(small, 1)
    merged = (middle.astype(F32) + ahead.astype(F32) * scales).astype(BF16)
    spots = [core * (size // 2), (1 - core) * (size // 2), start]
    left = next_left(left, spots, [small_in, places.core(small_in)], [part, places.core(part)])
    pieces, offsets = half_sweep(places, merged, left, right, half, side)
    (final_rows,) = truncate(pieces, offsets, c * (2 * half), rank, sketch_cols[0, 1], 2 * half, True)
    return final_rows[None]


def solution(mesh):
    places = Places(mesh)

    def run(*arrays):
        return on_device(places, *arrays)

    return jax.shard_map(
        run,
        mesh=mesh,
        in_specs=(
            P("seg", "sec", None),
            P("seg", "mpo", "sec", None),
            P("seg", "mpo", None, None),
            P("seg", None),
            P("seg", None, None, None),
            P("seg"),
        ),
        out_specs=P("seg", "sec", None),
        check_vma=False,
    )
```
